32 devices in a mesh: rep: 8 (over z, y), grp: 4 (over x, core).
Axes of the slice: x: 2, y: 2, z: 4, core: 2. Of those that a mesh axis runs over, the one named last changes fastest.
Arguments:
- block_input: bfloat16 [8, 768, 1152], P('rep', 'grp'), may hold values from -6 to 6
- lengths: int32 [8], P('rep'), may hold values from 384 to 768, as said below
- ln1_gain: bfloat16 [1152], P('grp'), may hold values from 0.5 to 1.5
- ln1_bias: bfloat16 [1152], P('grp'), may hold values from -3 to 3
- w_qkv: bfloat16 [1152, 3456], P('grp'), as said below
- b_qv: bfloat16 [2304], P('grp'), may hold values from -3 to 3
- w_out: bfloat16 [1152, 1152], P('grp'), may hold values from -3.5 to 3.5
- b_out: bfloat16 [1152], P('grp'), may hold values from -3 to 3
- ln2_gain: bfloat16 [1152], P('grp'), may hold values from 0.5 to 1.5
- ln2_bias: bfloat16 [1152], P('grp'), may hold values from -3 to 3
- w_up: bfloat16 [1152, 4304], P(None, 'grp'), may hold values from -0.1875 to 0.1875
- b_up: bfloat16 [4304], P('grp'), may hold values from -3 to 3
- w_down: bfloat16 [4304, 1152], P('grp'), may hold values from -0.09375 to 0.09375
- b_down: bfloat16 [1152], P('grp'), may hold values from -3 to 3
- cotangent: bfloat16 [8, 768, 1152], P('rep', 'grp'), may hold values from -6 to 6
Outputs:
- block_output: bfloat16 [8, 768, 1152], P('rep', 'grp')
- grad_input: bfloat16 [8, 768, 1152], P('rep', 'grp')
- grad_ln1_gain: float32 [1152], P('grp')
- grad_ln1_bias: float32 [1152], P('grp')
- grad_w_qkv: float32 [1152, 3456], P('grp', 'rep')
- grad_b_qv: float32 [2304], P('grp')
- grad_w_out: float32 [1152, 1152], P('grp', 'rep')
- grad_b_out: float32 [1152], P('grp')
- grad_ln2_gain: float32 [1152], P('grp')
- grad_ln2_bias: float32 [1152], P('grp')
- grad_w_up: float32 [1152, 4304], P('rep', 'grp')
- grad_b_up: float32 [4304], P('grp')
- grad_w_down: float32 [4304, 1152], P('grp', 'rep')
- grad_b_down: float32 [1152], P('grp')
The draws below stay inside these ranges and needn't reach their ends.
Inputs may be any that keep to these rules, and one draw needn't show every extreme that they name: `lengths`: valid tokens of each image, counted from its first slot. `w_qkv`: query, key and value projections in this column order.
All inputs are finite; a program needn't handle non-finite values.
Results may differ from the reference program's by a relative error of at most 0.012.
Values may be sent and summed in bfloat16 or wider, within the bound.
No kernel may reach another device: no remote copies, remote signals or barrier semaphores. Data moves between devices by JAX's collectives and lax.ppermute only.
A program may use at most 192 MiB of HBM per device.

```python
import math
import jax
import jax.numpy as jnp
from jax import lax

D = 1152
HEADS = 16
MLP = 4304
SEQ = 768
IMAGES = 8


def draw_lengths(key, part):
    first_key, second_key, third_key = jax.random.split(key, 3)
    counts = jax.random.randint(first_key, (IMAGES,), SEQ // 2, SEQ + 1)
    longest = jax.random.randint(second_key, (), 0, IMAGES)
    shortest = (longest + jax.random.randint(third_key, (), 1, IMAGES)) % IMAGES
    counts = counts.at[longest].set(SEQ).at[shortest].set(SEQ // 2)
    return counts.astype(jnp.int32)


def draw_w_qkv(key, part):
    base_key = jax.random.fold_in(key, 0)
    base = jax.random.normal(base_key, (D, 3 * D), jnp.float32) / math.sqrt(D)
    return base.astype(jnp.bfloat16)


def shard_levels(key, dims, cuts, least, top_value):
    loudness = 1.0
    for dim, parts in cuts:
        draws = jax.random.uniform(jax.random.fold_in(jax.random.fold_in(key, 6), dim), (parts,), jnp.float32, least / len(cuts), top_value / len(cuts))
        loudness = loudness * jnp.repeat(jnp.exp(draws), dims[dim] // parts).reshape((-1,) + (1,) * (len(dims) - 1 - dim))
    return loudness


def bell_draw(rng, shape, deviation, reach, cuts=(), kind=jnp.bfloat16):
    level = shard_levels(rng, shape, cuts, -0.22, 0.18) if cuts else 1.0
    array = jax.random.normal(rng, shape, jnp.float32) * deviation * level
    return jnp.minimum(jnp.maximum(array, -reach), reach).astype(kind)


def setup_inputs(seed: int = 0) -> dict:
    arg_keys = jax.random.split(jax.random.key(seed), 16)
    block_input = bell_draw(arg_keys[0], (IMAGES, SEQ, D), 1.0, 6.0, ((0, 8), (1, 4)))
    lengths = draw_lengths(jax.random.fold_in(arg_keys[15], 71), 0)
    ln1_gain = jnp.clip(1.0 + 0.1 * jax.random.normal(arg_keys[2], (D,), jnp.float32), 0.5, 1.5).astype(jnp.bfloat16)
    ln1_bias = bell_draw(arg_keys[3], (D,), 0.5, 3.0, ((0, 4),))
    w_qkv = draw_w_qkv(jax.random.fold_in(arg_keys[15], 71), 0)
    b_qv = bell_draw(arg_keys[5], (2 * D,), 0.5, 3.0, ((0, 4),))
    w_out = bell_draw(arg_keys[6], (D, D), (max(2 * D // SEQ, 1)) ** -0.5, 3.5, ((0, 4),))
    b_out = bell_draw(arg_keys[7], (D,), 0.5, 3.0, ((0, 4),))
    ln2_gain = jnp.clip(1.0 + 0.1 * jax.random.normal(arg_keys[8], (D,), jnp.float32), 0.5, 1.5).astype(jnp.bfloat16)
    ln2_bias = bell_draw(arg_keys[9], (D,), 0.5, 3.0, ((0, 4),))
    w_up = bell_draw(arg_keys[10], (D, MLP), D ** -0.5, 0.1875, ((1, 4),))
    b_up = bell_draw(arg_keys[11], (MLP,), 0.5, 3.0, ((0, 4),))
    w_down = bell_draw(arg_keys[12], (MLP, D), MLP ** -0.5, 0.09375, ((0, 4),))
    b_down = bell_draw(arg_keys[13], (D,), 0.5, 3.0, ((0, 4),))
    cotangent = bell_draw(arg_keys[14], (IMAGES, SEQ, D), 1.0, 6.0, ((0, 8), (1, 4)))
    return dict(block_input=block_input, lengths=lengths, ln1_gain=ln1_gain, ln1_bias=ln1_bias, w_qkv=w_qkv, b_qv=b_qv, w_out=w_out, b_out=b_out, ln2_gain=ln2_gain, ln2_bias=ln2_bias, w_up=w_up, b_up=b_up, w_down=w_down, b_down=b_down, cotangent=cotangent)


EPSILON = 1e-06
GELU_SCALE = 0.7978845608028654
GELU_CUBIC = 0.044715
NEG_FILL = -1000000000.0

def layer_norm(values, gain, shift):
    center = values - lax.optimization_barrier(jnp.mean(values, axis=-1, keepdims=True))
    inv_std = lax.rsqrt(lax.optimization_barrier(jnp.mean(center * center, axis=-1, keepdims=True)) + EPSILON)
    normed = center * inv_std
    return (normed * gain + shift, normed, inv_std)

def norm_backward(upstream, normed, inv_std, gain):
    scaled = upstream * gain
    return inv_std * (scaled - lax.optimization_barrier(jnp.mean(scaled, axis=-1, keepdims=True)) - normed * lax.optimization_barrier(jnp.mean(scaled * normed, axis=-1, keepdims=True)))

def gelu_with_slope(values):
    cubic = values * values * values
    tangent = jnp.tanh(GELU_SCALE * (values + GELU_CUBIC * cubic))
    output = 0.5 * values * (1.0 + tangent)
    slope = 0.5 * (1.0 + tangent) + 0.5 * values * (1.0 - tangent * tangent) * GELU_SCALE * (1.0 + 3.0 * GELU_CUBIC * values * values)
    return (output, slope)

def split_heads(rows):
    return rows.astype(jnp.float32).reshape(rows.shape[0], HEADS, rows.shape[1] // HEADS)

def image_pass(image_in, valid_count, upstream, params):
    ln1_gain, ln1_bias, w_qkv, b_qv, w_out, b_out, ln2_gain, ln2_bias, w_up, b_up, w_down, b_down = params
    seq_len = image_in.shape[0]
    model_width = image_in.shape[1]
    score_scale = 1.0 / math.sqrt(model_width // HEADS)
    residual_in = image_in.astype(jnp.float32)
    normed_out, normed_one, inv_one = layer_norm(residual_in, ln1_gain.astype(jnp.float32), ln1_bias.astype(jnp.float32))
    first_input = normed_out.astype(jnp.bfloat16)
    projected = jnp.dot(first_input, w_qkv, preferred_element_type=jnp.float32)
    bias_wide = b_qv.astype(jnp.float32)
    queries = (projected[:, :model_width] + bias_wide[:model_width]).astype(jnp.bfloat16)
    key_rows = projected[:, model_width:2 * model_width].astype(jnp.bfloat16)
    value_rows = (projected[:, 2 * model_width:] + bias_wide[model_width:]).astype(jnp.bfloat16)
    live = jnp.arange(seq_len) < valid_count
    query_heads = split_heads(queries)
    key_heads = split_heads(key_rows)
    value_heads = split_heads(value_rows)
    scores = jnp.einsum('qhd,khd->hqk', query_heads, key_heads) * score_scale
    scores = jnp.where(live[None, None, :], scores, NEG_FILL)
    top = lax.optimization_barrier(jnp.max(scores, axis=-1, keepdims=True))
    log_total = top + jnp.log(lax.optimization_barrier(jnp.sum(jnp.exp(scores - top), axis=-1, keepdims=True)))
    probs_wide = jnp.exp(scores - log_total)
    probs = probs_wide.astype(jnp.bfloat16)
    mixed = jnp.einsum('hqk,khd->qhd', probs.astype(jnp.float32), value_heads)
    mixed = mixed.reshape(seq_len, model_width).astype(jnp.bfloat16)
    residual_mid = residual_in + (jnp.dot(mixed, w_out, preferred_element_type=jnp.float32) + b_out.astype(jnp.float32))
    normed_out2, normed_two, inv_two = layer_norm(residual_mid, ln2_gain.astype(jnp.float32), ln2_bias.astype(jnp.float32))
    second_input = normed_out2.astype(jnp.bfloat16)
    pre_act = jnp.dot(second_input, w_up, preferred_element_type=jnp.float32) + b_up.astype(jnp.float32)
    activated_wide, slope = gelu_with_slope(pre_act)
    activated = activated_wide.astype(jnp.bfloat16)
    block_rows = residual_mid + (jnp.dot(activated, w_down, preferred_element_type=jnp.float32) + b_down.astype(jnp.float32))
    block_output = block_rows.astype(jnp.bfloat16)
    upstream_wide = upstream.astype(jnp.float32)
    grad_w_down = jnp.dot(activated.T, upstream, preferred_element_type=jnp.float32)
    grad_b_down = lax.optimization_barrier(jnp.sum(upstream_wide, axis=0))
    gate_grad = jnp.dot(upstream, w_down.T, preferred_element_type=jnp.float32) * slope
    gate_low = gate_grad.astype(jnp.bfloat16)
    grad_w_up = jnp.dot(second_input.T, gate_low, preferred_element_type=jnp.float32)
    grad_b_up = lax.optimization_barrier(jnp.sum(gate_grad, axis=0))
    grad_second = jnp.dot(gate_low, w_up.T, preferred_element_type=jnp.float32)
    grad_ln2_gain = lax.optimization_barrier(jnp.sum(grad_second * normed_two, axis=0))
    grad_ln2_bias = lax.optimization_barrier(jnp.sum(grad_second, axis=0))
    grad_mid = upstream_wide + norm_backward(grad_second, normed_two, inv_two, ln2_gain.astype(jnp.float32))
    grad_mid_low = grad_mid.astype(jnp.bfloat16)
    grad_w_out = jnp.dot(mixed.T, grad_mid_low, preferred_element_type=jnp.float32)
    grad_b_out = lax.optimization_barrier(jnp.sum(grad_mid, axis=0))
    grad_mixed = jnp.dot(grad_mid_low, w_out.T, preferred_element_type=jnp.float32).astype(jnp.bfloat16)
    grad_heads = split_heads(grad_mixed)
    dprob = jnp.einsum('qhd,khd->hqk', grad_heads, value_heads)
    delta = lax.optimization_barrier(jnp.sum(probs_wide * dprob, axis=-1, keepdims=True))
    dscore = (probs_wide * (dprob - delta) * score_scale).astype(jnp.bfloat16).astype(jnp.float32)
    grad_query = jnp.einsum('hqk,khd->qhd', dscore, key_heads).reshape(seq_len, model_width)
    grad_key = jnp.einsum('hqk,qhd->khd', dscore, query_heads).reshape(seq_len, model_width)
    grad_value = jnp.einsum('hqk,qhd->khd', probs.astype(jnp.float32), grad_heads).reshape(seq_len, model_width)
    grad_proj = jnp.concatenate([grad_query, grad_key, grad_value], axis=1).astype(jnp.bfloat16)
    grad_w_qkv = jnp.dot(first_input.T, grad_proj, preferred_element_type=jnp.float32)
    grad_b_qv = jnp.concatenate([lax.optimization_barrier(jnp.sum(grad_query, axis=0)), lax.optimization_barrier(jnp.sum(grad_value, axis=0))])
    grad_first = jnp.dot(grad_proj, w_qkv.T, preferred_element_type=jnp.float32)
    grad_ln1_gain = lax.optimization_barrier(jnp.sum(grad_first * normed_one, axis=0))
    grad_ln1_bias = lax.optimization_barrier(jnp.sum(grad_first, axis=0))
    grad_input = (grad_mid + norm_backward(grad_first, normed_one, inv_one, ln1_gain.astype(jnp.float32))).astype(jnp.bfloat16)
    grads = (grad_ln1_gain, grad_ln1_bias, grad_w_qkv, grad_b_qv, grad_w_out, grad_b_out, grad_ln2_gain, grad_ln2_bias, grad_w_up, grad_b_up, grad_w_down, grad_b_down)
    return (block_output, grad_input, grads)

def reference(block_input, lengths, ln1_gain, ln1_bias, w_qkv, b_qv, w_out, b_out, ln2_gain, ln2_bias, w_up, b_up, w_down, b_down, cotangent):
    params = (ln1_gain, ln1_bias, w_qkv, b_qv, w_out, b_out, ln2_gain, ln2_bias, w_up, b_up, w_down, b_down)
    starting = tuple((jnp.zeros(param.shape, jnp.float32) for param in params))

    def per_image(totals, item):
        image_in, valid_count, upstream = item
        block_output, grad_input, grads = image_pass(image_in, valid_count, upstream, params)
        return (tuple((total + term for total, term in zip(totals, grads))), (block_output, grad_input))
    totals, stacked = lax.scan(per_image, starting, (block_input, lengths, cotangent))
    return (stacked[0], stacked[1], totals[0], totals[1], totals[2], totals[3], totals[4], totals[5], totals[6], totals[7], totals[8], totals[9], totals[10], totals[11])
```

```python
import math

import jax
import jax.numpy as jnp
from jax import lax
from jax.sharding import PartitionSpec as P

HEADS = 16


EPSILON = 1e-06
GELU_SCALE = 0.7978845608028654
GELU_CUBIC = 0.044715
NEG_FILL = -1000000000.0


def layer_norm(values, gain, shift):
    center = values - jnp.mean(values, axis=-1, keepdims=True)
    inv_std = lax.rsqrt(jnp.mean(center * center, axis=-1, keepdims=True) + EPSILON)
    normed = center * inv_std
    return (normed * gain + shift, normed, inv_std)


def norm_backward(upstream, normed, inv_std, gain):
    scaled = upstream * gain
    return inv_std * (
        scaled
        - jnp.mean(scaled, axis=-1, keepdims=True)
        - normed * jnp.mean(scaled * normed, axis=-1, keepdims=True)
    )


def gelu_with_slope(values):
    cubic = values * values * values
    tangent = jnp.tanh(GELU_SCALE * (values + GELU_CUBIC * cubic))
    output = 0.5 * values * (1.0 + tangent)
    slope = 0.5 * (1.0 + tangent) + 0.5 * values * (1.0 - tangent * tangent) * GELU_SCALE * (
        1.0 + 3.0 * GELU_CUBIC * values * values
    )
    return (output, slope)


def xor_perm(size, bit):
    return [(i, i ^ bit) for i in range(size)]


def swap(values, axis, bit):
    return lax.ppermute(values, axis, xor_perm(lax.axis_size(axis), bit))


def low(values):
    return values.astype(jnp.bfloat16)


def wide(values):
    return values.astype(jnp.float32)


def gather_near(own):
    across = swap(own, "grp", 2)
    beside = swap(own, "grp", 1)
    return [own, beside, across, swap(across, "grp", 1)]


def gather_mixed(own, block):
    got = gather_near(own)
    return [got[0]] + [turn_rows(got[r], r, block) for r in range(1, 4)]


def turn_rows(values, r, block):
    split = values.reshape(4, block, values.shape[1])
    return jnp.concatenate([split[s ^ r] for s in range(4)])


def scatter_near(parts):
    beside = swap(low(jnp.stack([parts[1], parts[3]])), "grp", 1)
    far = swap(low(parts[2] + wide(beside[1])), "grp", 2)
    return parts[0] + wide(beside[0]) + wide(far)


def halve_rep(rows):
    size = lax.axis_size("rep")
    bits = size.bit_length() - 1
    position = lax.axis_index("rep")
    current = rows.reshape((2,) * bits + (rows.shape[0] // size, rows.shape[1]))
    for level in range(bits):
        axis = bits - 1 - level
        mine = (position >> level) & 1
        sent = lax.dynamic_index_in_dim(current, 1 - mine, axis, keepdims=False)
        kept = lax.dynamic_index_in_dim(current, mine, axis, keepdims=False)
        current = wide(kept) + wide(swap(low(sent), "rep", 1 << level))
    return current


def sum_rep(values):
    size = lax.axis_size("rep")
    for level in range(size.bit_length() - 1):
        values = values + swap(values, "rep", 1 << level)
    return values


def on_device(
    block_input,
    lengths,
    ln1_gain,
    ln1_bias,
    w_qkv,
    b_qv,
    w_out,
    b_out,
    ln2_gain,
    ln2_bias,
    w_up,
    b_up,
    w_down,
    b_down,
    cotangent,
):
    images, tokens_here, width = block_input.shape
    group = lax.axis_size("grp")
    me = lax.axis_index("grp")
    order = me ^ jnp.arange(group)
    cols = width // group
    heads = HEADS // group
    dim = width // HEADS
    rows = group * tokens_here
    score_scale = 1.0 / math.sqrt(dim)

    def dot(a, b, dims):
        return lax.dot_general(a, b, (dims, ((), ())), preferred_element_type=jnp.float32)

    packed = jnp.concatenate([ln1_gain, ln1_bias, b_out, ln2_gain, ln2_bias, b_down, b_qv])
    packed_all = jnp.stack(gather_near(packed))[order]
    vecs = wide(packed_all[:, : 6 * cols].reshape(group, 6, cols).transpose(1, 0, 2).reshape(6, width))
    gain_one, shift_one, out_bias, gain_two, shift_two, down_bias = [vecs[i] for i in range(6)]
    qv_bias = wide(packed_all[:, 6 * cols :].reshape(2, group, cols)[:, me])

    x_all = jnp.concatenate(gather_near(block_input.reshape(tokens_here, width)))
    w_split = w_qkv.reshape(cols, 3, group, cols)
    pieces = [
        lax.dynamic_index_in_dim(w_split, me ^ r, 2, keepdims=False).reshape(cols, 3 * cols)
        for r in range(group)
    ]
    pieces = [pieces[0]] + [swap(pieces[r], "grp", r) for r in range(1, group)]
    wq_local = jnp.stack(pieces)[order].reshape(width, 3 * cols)
    up_all = jnp.concatenate(gather_near(cotangent.reshape(tokens_here, width)))
    w_out_rel = jnp.concatenate(gather_near(w_out))

    resid = wide(x_all)
    normed_out, normed_one, inv_one = layer_norm(resid, gain_one, shift_one)
    first_input = low(normed_out)
    projected = dot(first_input, wq_local, ((1,), (0,)))
    queries = low(projected[:, :cols] + qv_bias[0])
    key_rows = low(projected[:, cols : 2 * cols])
    value_rows = low(projected[:, 2 * cols :] + qv_bias[1])
    spot = jnp.arange(rows)
    spot = (me ^ (spot // tokens_here)) * tokens_here + spot % tokens_here
    live = spot < lengths[0]

    def split(values):
        return values.reshape(rows, heads, dim)

    qh, kh, vh = split(queries), split(key_rows), split(value_rows)
    scores = jnp.einsum("qhd,khd->hqk", qh, kh, preferred_element_type=jnp.float32) * score_scale
    scores = jnp.where(live[None, None, :], scores, NEG_FILL)
    top = jnp.max(scores, axis=-1, keepdims=True)
    log_total = top + jnp.log(jnp.sum(jnp.exp(scores - top), axis=-1, keepdims=True))
    probs_wide = jnp.exp(scores - log_total)
    probs = low(probs_wide)
    mixed = jnp.einsum("hqk,khd->qhd", probs, vh, preferred_element_type=jnp.float32)
    mixed = low(mixed.reshape(rows, cols))

    mixed_rel = jnp.concatenate(gather_mixed(mixed, tokens_here), axis=1)
    resid_mid = resid + (dot(mixed_rel, w_out_rel, ((1,), (0,))) + out_bias)
    normed_out2, normed_two, inv_two = layer_norm(resid_mid, gain_two, shift_two)
    second_input = low(normed_out2)
    pre_act = dot(second_input, w_up, ((1,), (0,))) + wide(b_up)
    act_wide, slope = gelu_with_slope(pre_act)
    activated = low(act_wide)
    gate_grad = dot(up_all, w_down, ((1,), (1,))) * slope
    gate_low = low(gate_grad)
    partial_back = dot(gate_low, w_up, ((1,), (1,)))
    grad_second = scatter_near(list(partial_back.reshape(group, tokens_here, width)))

    own = slice(0, tokens_here)
    up_own = wide(up_all[own])
    normed_two_own = normed_two[own]
    gain_two_term = jnp.sum(grad_second * normed_two_own, axis=0)
    shift_two_term = jnp.sum(grad_second, axis=0)
    grad_mid = up_own + norm_backward(grad_second, normed_two_own, inv_two[own], gain_two)
    out_bias_term = jnp.sum(grad_mid, axis=0)
    mid_all = jnp.concatenate(gather_near(low(grad_mid)))

    partial_rows = dot(activated, w_down, ((1,), (0,)))
    branch = scatter_near(list(partial_rows.reshape(group, tokens_here, width)))
    block_rows = resid_mid[own] + (branch + down_bias)
    down_grad = halve_rep(dot(up_all, activated, ((0,), (0,))))
    up_grad = halve_rep(dot(second_input, gate_low, ((0,), (0,))))
    up_bias_term = jnp.sum(gate_grad, axis=0)
    down_bias_term = jnp.sum(wide(up_all), axis=0)

    out_grad = halve_rep(dot(mid_all, mixed, ((0,), (0,))))
    grad_mixed = low(dot(mid_all, w_out, ((1,), (1,))))
    gh = split(grad_mixed)
    dprob = jnp.einsum("qhd,khd->hqk", gh, vh, preferred_element_type=jnp.float32)
    delta = jnp.sum(probs_wide * dprob, axis=-1, keepdims=True)
    dscore = low(probs_wide * (dprob - delta) * score_scale)
    grad_query = jnp.einsum("hqk,khd->qhd", dscore, kh, preferred_element_type=jnp.float32)
    grad_key = jnp.einsum("hqk,qhd->khd", dscore, qh, preferred_element_type=jnp.float32)
    grad_value = jnp.einsum("hqk,qhd->khd", probs, gh, preferred_element_type=jnp.float32)
    grad_query = grad_query.reshape(rows, cols)
    grad_value = grad_value.reshape(rows, cols)
    grad_proj = low(jnp.concatenate([grad_query, grad_key.reshape(rows, cols), grad_value], axis=1))
    grad_proj = lax.optimization_barrier(grad_proj)
    partial_first = lax.optimization_barrier(dot(grad_proj, wq_local, ((1,), (1,))))
    grad_first = scatter_near(list(partial_first.reshape(group, tokens_here, width)))
    grad_rows = grad_mid + norm_backward(grad_first, normed_one[own], inv_one[own], gain_one)

    first_split = first_input.reshape(rows, group, cols)
    qkv_parts = []
    for r in range(group):
        block = lax.dynamic_index_in_dim(first_split, me ^ r, 1, keepdims=False)
        part = low(dot(grad_proj, block, ((0,), (0,))))
        qkv_parts.append(swap(part, "grp", r) if r else part)
    qkv_rows = jnp.stack(qkv_parts)[order].reshape(group, 3, cols, cols)
    qkv_grad = halve_rep(qkv_rows.transpose(1, 0, 2, 3).reshape(3 * width, cols))

    gain_one_term = jnp.sum(partial_first * normed_one, axis=0)
    shift_one_term = jnp.sum(partial_first, axis=0)
    zeros = jnp.zeros((2, group, cols), jnp.float32)
    qv_term = jnp.stack([jnp.sum(grad_query, axis=0), jnp.sum(grad_value, axis=0)])
    qv_term = lax.dynamic_update_index_in_dim(zeros, qv_term[:, None], me, 1)
    stacked = jnp.concatenate(
        [
            term.reshape(group, cols)
            for term in (gain_one_term, shift_one_term, out_bias_term, gain_two_term, shift_two_term)
        ]
        + [qv_term.reshape(group, 2 * cols)],
        axis=1,
    )
    stacked = stacked[order]
    beside = swap(stacked[1::2], "grp", 1)
    pair = stacked[::2] + beside
    mine = pair[0] + swap(pair[1], "grp", 2)
    down_own = lax.dynamic_index_in_dim(down_bias_term.reshape(group, cols), me, 0, keepdims=False)
    summed = sum_rep(jnp.concatenate([mine, down_own, up_bias_term]))
    vec = [summed[i * cols : (i + 1) * cols] for i in range(5)]
    return (
        low(block_rows).reshape(block_input.shape),
        low(grad_rows).reshape(block_input.shape),
        vec[0],
        vec[1],
        qkv_grad.T,
        summed[5 * cols : 7 * cols],
        out_grad.T,
        vec[2],
        vec[3],
        vec[4],
        up_grad,
        summed[8 * cols :],
        down_grad.T,
        summed[7 * cols : 8 * cols],
    )


def solution(mesh):
    in_specs = (
        P("rep", "grp", None),
        P("rep"),
        P("grp"),
        P("grp"),
        P("grp", None),
        P("grp"),
        P("grp", None),
        P("grp"),
        P("grp"),
        P("grp"),
        P(None, "grp"),
        P("grp"),
        P("grp", None),
        P("grp"),
        P("rep", "grp", None),
    )
    out_specs = (
        P("rep", "grp", None),
        P("rep", "grp", None),
        P("grp"),
        P("grp"),
        P("grp", "rep"),
        P("grp"),
        P("grp", "rep"),
        P("grp"),
        P("grp"),
        P("grp"),
        P("rep", "grp"),
        P("grp"),
        P("grp", "rep"),
        P("grp"),
    )
    return jax.shard_map(
        on_device, mesh=mesh, in_specs=in_specs, out_specs=out_specs, check_vma=False
    )
```

```python
import functools
import math

import jax
import jax.numpy as jnp
from jax import lax
from jax.experimental import pallas as pl
from jax.experimental.pallas import tpu as pltpu
from jax.sharding import PartitionSpec as P

HEADS = 16


EPSILON = 1e-06
GELU_SCALE = 0.7978845608028654
GELU_CUBIC = 0.044715
NEG_FILL = -1000000000.0
BF = jnp.bfloat16
F32 = jnp.float32


def norm_stats(values):
    center = values - jnp.mean(values, axis=-1, keepdims=True)
    inv_std = lax.rsqrt(jnp.mean(center * center, axis=-1, keepdims=True) + EPSILON)
    return center * inv_std, inv_std


def norm_backward(upstream, normed, inv_std, gain):
    scaled = upstream * gain
    return inv_std * (
        scaled
        - jnp.mean(scaled, axis=-1, keepdims=True)
        - normed * jnp.mean(scaled * normed, axis=-1, keepdims=True)
    )


def gelu_with_slope(values):
    square = values * values
    tangent = jnp.tanh(GELU_SCALE * (values + GELU_CUBIC * (values * square)))
    half = 0.5 * (1.0 + tangent)
    slope = half + 0.5 * values * (1.0 - tangent * tangent) * GELU_SCALE * (
        1.0 + 3.0 * GELU_CUBIC * square
    )
    return (values * half, slope)


def low(values):
    return values.astype(BF)


def wide(values):
    return values.astype(F32)


def dot(a, b, dims):
    return lax.dot_general(a, b, (dims, ((), ())), preferred_element_type=F32)


NN = ((1,), (0,))
NT = ((1,), (1,))
TN = ((0,), (0,))


def xor_perm(size, bit):
    return [(i, i ^ bit) for i in range(size)]


def swap(values, axis, bit):
    return lax.ppermute(values, axis, xor_perm(lax.axis_size(axis), bit))


def gather_near(own):
    across = swap(own, "grp", 2)
    beside = swap(own, "grp", 1)
    return [own, beside, across, swap(across, "grp", 1)]


def local_call(body, outs, args, scratch=(), name=None):
    specs = [pl.BlockSpec(memory_space=pltpu.SMEM)]
    specs += [pl.BlockSpec(memory_space=pltpu.VMEM)] * (len(args) - 1)
    return pl.pallas_call(
        body,
        out_shape=[jax.ShapeDtypeStruct(shape, dtype) for shape, dtype in outs],
        in_specs=specs,
        out_specs=[pl.BlockSpec(memory_space=pltpu.VMEM)] * len(outs),
        scratch_shapes=list(scratch),
        compiler_params=pltpu.CompilerParams(vmem_limit_bytes=60000 * 1024),
        name=name,
    )(*args)


def unpack_body(info, p0, p1, p2, p3, vecs, bias, spread):
    me = info[0]
    cols = p0.shape[1]
    for r, piece in enumerate((p0, p1, p2, p3)):
        spread[me ^ r] = piece[...]
    for d in range(4):
        vecs[:, d * cols : (d + 1) * cols] = spread[d]
    odd = (me & 1) == 1
    for i in range(2):
        block = spread[2 * i + (me >> 1)]
        bias[i : i + 1, :] = jnp.where(odd, block[7:8, :], block[6:7, :])


def split_w_body(info, w, own, beside, far, flat):
    me, bit = info[0], info[2] & 1
    cols = flat.shape[1]
    half = cols // 2
    width = 4 * cols
    for d in range(4):
        parts = [w[:, j * width + d * cols : j * width + (d + 1) * cols] for j in range(3)]
        flat[me ^ d] = jnp.concatenate(parts, axis=1)
    start = pl.multiple_of(bit * half, 16)
    own[...] = flat[0]
    beside[:cols, :] = flat[1]
    beside[cols:, :] = flat[3, pl.ds(start, half), :]
    far[...] = flat[2, pl.ds(start, half), :]


def norm_one_body(info, x0, x1, x2, x3, vecs, first):
    block = x0.shape[0]
    step = 64
    for r, x in enumerate((x0, x1, x2, x3)):

        def rows(c, carry):
            start = pl.multiple_of(c * step, step)
            normed, _ = norm_stats(wide(x[pl.ds(start, step), :]))
            first[pl.ds(r * block + start, step), :] = low(normed * vecs[0:1, :] + vecs[1:2, :])
            return carry

        lax.fori_loop(0, block // step, rows, 0)


def attend_body(info, first, w0, w1, w2, w3, bias, wq, qs, ks, vs, probs, mixed, ms):
    bit = info[2] & 1
    me, length = info[0], info[1]
    cols = w0.shape[0]
    rows = first.shape[0]
    heads, _, dim = qs.shape
    half = cols // 2
    wq[pl.ds(pl.multiple_of(me * cols, 16), cols), :] = w0[...]
    wq[pl.ds(pl.multiple_of((me ^ 1) * cols, 16), cols), :] = w1[:cols, :]
    for w, side in ((w2, bit), (w3, 1 - bit)):
        for r in (2, 3):
            start = pl.multiple_of((me ^ r) * cols + side * half, 16)
            wq[pl.ds(start, half), :] = w[(r - 2) * half : (r - 1) * half, :]
    for j, (out, shift) in enumerate(((qs, 0), (ks, None), (vs, 1))):
        part = dot(first[...], wq[:, j * cols : (j + 1) * cols], NN)
        if shift is not None:
            part = part + bias[shift : shift + 1, :]
        part = low(part)
        for h in range(heads):
            out[h] = part[:, h * dim : (h + 1) * dim]
    block = rows // 4
    spot = lax.broadcasted_iota(jnp.int32, (1, rows), 1)
    near = spot // block
    live = ((me ^ near) * block + (spot - near * block)) < length
    scale = 1.0 / math.sqrt(dim)
    step = 256

    def one(i, carry):
        h = i // (rows // step)
        start = pl.multiple_of((i % (rows // step)) * step, step)
        scores = dot(qs[h, pl.ds(start, step), :], ks[h], NT) * scale
        scores = jnp.where(live, scores, NEG_FILL)
        top = jnp.max(scores, axis=-1, keepdims=True)
        raised = jnp.exp(scores - top)
        share = low(raised * (1.0 / jnp.sum(raised, axis=-1, keepdims=True)))
        probs[h, pl.ds(start, step), :] = share
        ms[h, pl.ds(start, step), :] = low(dot(share, vs[h], NN))
        return carry

    lax.fori_loop(0, heads * (rows // step), one, 0)
    for t in range(4):
        parts = [ms[h, t * block : (t + 1) * block, :] for h in range(heads)]
        mixed[:, t * cols : (t + 1) * cols] = jnp.concatenate(parts, axis=1)


def mlp_body(
    blocks, keep, info, m0, m1, m2, m3, o0, o1, o2, o2b, o3, o3b, xa, xb, ca, cb, vecs, w_up, b_up, w_down,
    second, activated, gate_low, back, gate_sum, cot_sum, *rest
):
    w_far = rest[-1]
    block = xa.shape[0]
    cols = o0.shape[0]
    half = cols // 2
    bit = info[2] & 1
    for i, (w, side) in enumerate(((o2, bit), (o2b, 1 - bit), (o3, bit), (o3b, 1 - bit))):
        start = pl.multiple_of((i // 2) * cols + side * half, 16)
        w_far[pl.ds(start, half), :] = w[...]
    total = None
    for r, m in enumerate((m0, m1, m2, m3)):
        lhs = jnp.concatenate(
            [m[:, (b ^ r) * cols : ((b ^ r) + 1) * cols] for b in blocks], axis=0
        )
        if r < 2:
            w = (o0, o1)[r][...]
        else:
            w = w_far[(r - 2) * cols : (r - 1) * cols, :]
        term = dot(lhs, w, NN)
        total = term if total is None else total + term
    resid = jnp.concatenate([wide(xa[...]), wide(xb[...])], axis=0) + (total + vecs[2:3, :])
    normed, _ = norm_stats(resid)
    second[...] = low(normed * vecs[3:4, :] + vecs[4:5, :])
    if keep:
        rest[0][...] = resid[:block, :]
    cot = jnp.concatenate([ca[...], cb[...]], axis=0)
    cot_sum[...] = jnp.sum(wide(cot), axis=0, keepdims=True)
    act, slope = gelu_with_slope(dot(second[...], w_up[...], NT) + wide(b_up[...]))
    activated[...] = low(act)
    gate = dot(cot, w_down[...], NT) * slope
    gate_sum[...] = jnp.sum(gate, axis=0, keepdims=True)
    gate_low[...] = low(gate)
    back[...] = dot(gate_low[...], w_up[...], NN).astype(back.dtype)


def forward_body(info, act_s, act_k, w_down, sent, kept):
    sent[...] = low(dot(act_s[...], w_down[...], NN))
    kept[...] = dot(act_k[...], w_down[...], NN)


def chunk_index(i, level, bit):
    return ((i >> level) << (level + 1)) | (bit << level) | (i & ((1 << level) - 1))


def split_halves(chunks, kept, sent, level, position):
    mine = (position >> level) & 1
    for i in range(kept.shape[0]):
        kept[i] = chunks[chunk_index(i, level, mine)]
        sent[i] = chunks[chunk_index(i, level, 1 - mine)]


def weight_body(level, info, *refs):
    kept, sent, chunks = refs[-3:]
    a = [r[...] for r in refs[: len(refs) - 3] if r.shape[1] == refs[0].shape[1]]
    b = [r[...] for r in refs[: len(refs) - 3] if r.shape[1] != refs[0].shape[1]]
    full = low(dot(jnp.concatenate(a, axis=0), jnp.concatenate(b, axis=0), TN))
    size, rows, _ = chunks.shape
    for c in range(size):
        chunks[c] = full[c * rows : (c + 1) * rows, :]
    split_halves(chunks, kept, sent, level, info[2])


def out_grad_body(info, g0, g1, g2, g3, mixed, out):
    cols = out.shape[1]
    a = jnp.concatenate([g0[...], g1[...], g2[...], g3[...]], axis=0)
    b = jnp.concatenate([mixed[:, t * cols : (t + 1) * cols] for t in range(4)], axis=0)
    out[...] = low(dot(a, b, TN))


def assemble_body(info, *refs):
    me = info[0]
    v, qk, out_full = refs[0:4], refs[4:8], refs[8]
    kept_a, sent_a, kept_b, sent_b, flat, part_a, part_b = refs[9:]
    cols = flat.shape[1]
    half = cols // 2
    width = 4 * cols
    for r in range(4):
        for t in range(4):
            start = pl.multiple_of((t // 2) * width + (me ^ r) * cols + (t % 2) * half, 16)
            flat[pl.ds(start, half), :] = qk[r][:, t * cols : (t + 1) * cols]
        flat[pl.ds(pl.multiple_of(2 * width + (me ^ r) * cols, 16), cols), :] = v[r][...]
    size, top, _ = part_a.shape
    sub = top + part_b.shape[1]
    for c in range(size):
        for b in range(4):
            lanes = slice(b * cols, (b + 1) * cols)
            source, start = (out_full, c * sub) if b == 3 else (flat, (3 * c + b) * sub)
            part_a[c, :, lanes] = source[start : start + top, :]
            part_b[c, :, lanes] = source[start + top : start + sub, :]
    split_halves(part_a, kept_a, sent_a, 0, info[2])
    split_halves(part_b, kept_b, sent_b, 1, info[2])


def finish_body(info, kept_a, got_a, kept_b, got_b, qkv, out):
    total = jnp.concatenate(
        [wide(kept_a[...]) + wide(got_a[...]), wide(kept_b[...]) + wide(got_b[...])], axis=0
    )
    cols = out.shape[1]
    turned = [total[:, b * cols : (b + 1) * cols].T for b in range(3)]
    qkv[...] = jnp.concatenate(turned, axis=1)
    out[...] = total[:, 3 * cols :]


def vectors_body(info, one, mid, q_sum, v_sum, cot_a, cot_b, kept, sent, spread):
    me = info[0]
    cols = q_sum.shape[1]
    cot = 0.25 * (cot_a[...] + cot_b[...])
    spread[...] = jnp.zeros_like(spread)
    for d in range(4):
        lanes = slice(d * cols, (d + 1) * cols)
        spread[d, 0:2, :] = one[:, lanes]
        spread[d, 2:5, :] = mid[:, lanes]
        spread[d, 7:8, :] = cot[:, lanes]
    row = lax.broadcasted_iota(jnp.int32, (2, cols), 0)
    spread[me >> 1, 5:7, :] = jnp.where(row == (me & 1), q_sum[...], 0.0)
    spread[2 + (me >> 1), 5:7, :] = jnp.where(row == (me & 1), v_sum[...], 0.0)
    for i in range(2):
        kept[i] = spread[me ^ (2 * i)]
        sent[i] = spread[me ^ (2 * i + 1)]


def norm_two_back_body(info, kept, beside, far, resid, cot, vecs, grad_mid, mid_low, sums):
    block = resid.shape[0]
    grad_second = kept[:block, :] + wide(beside[:block, :]) + wide(far[...])
    normed, inv = norm_stats(resid[...])
    grad = wide(cot[...]) + norm_backward(grad_second, normed, inv, vecs[3:4, :])
    grad_mid[...] = grad
    mid_low[...] = low(grad)
    sums[0:1, :] = jnp.sum(grad, axis=0, keepdims=True)
    sums[1:2, :] = jnp.sum(grad_second * normed, axis=0, keepdims=True)
    sums[2:3, :] = jnp.sum(grad_second, axis=0, keepdims=True)


def value_back_body(
    info, g0, g1, g2, g3, w_out, probs, first, gs, grad_v, v_sum, o0, o1, o2, o3, mid, vacc, flat, pieces
):
    me = info[0]
    block = g0.shape[0]
    heads, rows, dim = gs.shape
    cols = heads * dim
    for r, g in enumerate((g0, g1, g2, g3)):
        mid[r * block : (r + 1) * block, :] = g[...]
    grad_mixed = low(dot(mid[...], w_out[...], NT))
    for h in range(heads):
        gs[h] = grad_mixed[:, h * dim : (h + 1) * dim]

    def one(h, carry):
        vacc[h] = dot(probs[h], gs[h], TN)
        return carry

    lax.fori_loop(0, heads, one, 0)
    grad = jnp.concatenate([vacc[h] for h in range(heads)], axis=1)
    v_sum[...] = jnp.sum(grad, axis=0, keepdims=True)
    grad_v[...] = low(grad)
    flat[...] = low(dot(grad_v[...], first[...], TN))
    for d in range(4):
        pieces[me ^ d] = flat[:, d * cols : (d + 1) * cols]
    for r, out in enumerate((o0, o1, o2, o3)):
        out[...] = pieces[r]


def query_back_body(info, gs, vs, ks, qs, probs, grad_q, grad_k, q_sum, qacc, kacc):
    heads, rows, dim = gs.shape
    scale = 1.0 / math.sqrt(dim)
    step = 256
    kacc[...] = jnp.zeros_like(kacc)

    def one(i, carry):
        h = i // (rows // step)
        start = pl.multiple_of((i % (rows // step)) * step, step)
        here = pl.ds(start, step)
        g = gs[h, here, :]
        share = wide(probs[h, here, :])
        dprob = dot(g, vs[h], NT)
        delta = jnp.sum(share * dprob, axis=-1, keepdims=True)
        dscore = low(share * (dprob - delta) * scale)
        qacc[h, here, :] = dot(dscore, ks[h], NN)
        kacc[h] += dot(dscore, qs[h, here, :], TN)
        return carry

    lax.fori_loop(0, heads * (rows // step), one, 0)
    grad = jnp.concatenate([qacc[h] for h in range(heads)], axis=1)
    q_sum[...] = jnp.sum(grad, axis=0, keepdims=True)
    grad_q[...] = low(grad)
    grad_k[...] = low(jnp.concatenate([kacc[h] for h in range(heads)], axis=1))


def pieces_body(info, grad_a, grad_b, first, o0, o1, o2, o3, flat, pieces):
    me = info[0]
    cols = grad_a.shape[1]
    half = cols // 2
    for j, grad in enumerate((grad_a, grad_b)):
        flat[...] = low(dot(grad[...], first[...], TN))
        for d in range(4):
            for t in range(2):
                pieces[me ^ d, :, (2 * j + t) * cols : (2 * j + t + 1) * cols] = flat[
                    t * half : (t + 1) * half, d * cols : (d + 1) * cols
                ]
    for r, out in enumerate((o0, o1, o2, o3)):
        out[...] = pieces[r]


def first_back_body(info, grad_q, grad_k, grad_v, wq, x0, x1, x2, x3, kept, sent, sums):
    cols = grad_q.shape[1]
    block = x0.shape[0]
    total = None
    for j, grad in enumerate((grad_q, grad_k, grad_v)):
        term = dot(grad[...], wq[:, j * cols : (j + 1) * cols], NT)
        total = term if total is None else total + term
    gain = shift = 0.0
    for r, x in enumerate((x0, x1, x2, x3)):
        part = total[r * block : (r + 1) * block, :]
        normed, _ = norm_stats(wide(x[...]))
        gain = gain + jnp.sum(part * normed, axis=0, keepdims=True)
        shift = shift + jnp.sum(part, axis=0, keepdims=True)
        place = slice((r // 2) * block, (r // 2 + 1) * block)
        if r % 2:
            sent[place, :] = low(part)
        else:
            kept[place, :] = part
    sums[0:1, :] = gain
    sums[1:2, :] = shift


def norm_one_back_body(info, kept, beside, far, x, grad_mid, vecs, out):
    block = x.shape[0]
    normed, inv = norm_stats(wide(x[...]))
    grad_first = kept[:block, :] + wide(beside[:block, :]) + wide(far[...])
    out[...] = low(grad_mid[...] + norm_backward(grad_first, normed, inv, vecs[0:1, :]))


def scatter_near(kept, sent):
    block = kept.shape[0] // 2
    beside = swap(sent, "grp", 1)
    return beside, swap(low(kept[block:] + wide(beside[block:])), "grp", 2)


def after(values, *others):
    return lax.optimization_barrier((values,) + others)[0]


def rep_bits():
    return lax.axis_size("rep").bit_length() - 1


def halve_rest(kept, got, order):
    left = sorted(order)
    left.remove(order[0])
    kept = kept.reshape((2,) * len(left) + kept.shape[1:])
    got = got.reshape(kept.shape)
    for level in order[1:]:
        mine = (lax.axis_index("rep") >> level) & 1
        axis = len(left) - 1 - left.index(level)
        left.remove(level)

        def pick(values, bit):
            return wide(lax.dynamic_index_in_dim(values, bit, axis, keepdims=False))

        got_next = swap(low(pick(kept, 1 - mine) + pick(got, 1 - mine)), "rep", 1 << level)
        kept = pick(kept, mine) + pick(got, mine)
        got = got_next
    return kept, got


def on_device(
    block_input,
    lengths,
    ln1_gain,
    ln1_bias,
    w_qkv,
    b_qv,
    w_out,
    b_out,
    ln2_gain,
    ln2_bias,
    w_up,
    b_up,
    w_down,
    b_down,
    cotangent,
):
    images, block, width = block_input.shape
    group = lax.axis_size("grp")
    assert images == 1 and group == 4
    me = lax.axis_index("grp")
    order = me ^ jnp.arange(group)
    cols = width // group
    heads = HEADS // group
    dim = width // HEADS
    rows = group * block
    hidden = w_up.shape[1]
    info = jnp.stack([me.astype(jnp.int32), lengths[0], lax.axis_index("rep").astype(jnp.int32)])

    x_near = gather_near(block_input.reshape(block, width))
    half = cols // 2
    w_own, w_beside, w_far = local_call(
        split_w_body,
        [((cols, 3 * cols), BF), ((cols + half, 3 * cols), BF), ((half, 3 * cols), BF)],
        [info, w_qkv],
        [pltpu.VMEM((group, cols, 3 * cols), BF)],
        name="split_w",
    )
    w_beside = swap(w_beside, "grp", 1)
    w_across = swap(jnp.concatenate([w_far, w_beside[cols:]]), "grp", 2)
    w_near = [w_own, w_beside, w_across, swap(w_across, "rep", 1)]
    small = [after(ln1_gain, w_own), ln1_bias, b_out, ln2_gain, ln2_bias, b_down]
    packed = jnp.concatenate([wide(v) for v in small] + [wide(b_qv)]).reshape(8, cols)
    vecs, qv_bias = local_call(
        unpack_body,
        [((8, width), F32), ((2, cols), F32)],
        [info] + gather_near(packed),
        [pltpu.VMEM((group, 8, cols), F32)],
        name="unpack",
    )
    cot_near = gather_near(cotangent.reshape(block, width))
    side = lax.axis_index("rep") & 1
    out_half = swap(lax.dynamic_slice_in_dim(w_out, side * half, half, 0), "grp", 2)
    out_other = swap(out_half, "rep", 1)
    out_near = [w_out, swap(w_out, "grp", 1), out_half, out_other]
    out_near += [swap(out_half, "grp", 1), swap(out_other, "grp", 1)]

    (first,) = local_call(
        norm_one_body, [((rows, width), BF)], [info] + x_near + [vecs], name="norm_one"
    )
    head_shape = ((heads, rows, dim), BF)
    wq, qs, ks, vs, probs, mixed = local_call(
        attend_body,
        [((width, 3 * cols), BF), head_shape, head_shape, head_shape]
        + [((heads, rows, rows), BF), ((block, width), BF)],
        [info, first] + w_near + [qv_bias],
        [pltpu.VMEM((heads, rows, dim), BF)],
        name="attend",
    )

    mixed_near = gather_near(mixed)

    def mlp(blocks, keep):
        kind = F32 if keep else BF
        outs = [((2 * block, width), BF), ((2 * block, hidden), BF), ((2 * block, hidden), BF)]
        outs += [((2 * block, width), kind)]
        outs += [((1, hidden), F32), ((1, width), F32)]
        if keep:
            outs += [((block, width), F32)]
        args = [info] + mixed_near + out_near + [x_near[b] for b in blocks]
        args += [cot_near[b] for b in blocks] + [vecs, w_up.T, b_up.reshape(1, -1), w_down]
        return local_call(
            functools.partial(mlp_body, blocks, keep),
            outs,
            args,
            [pltpu.VMEM((2 * cols, width), BF)],
            name="mlp",
        )

    size = lax.axis_size("rep")
    forth = list(range(rep_bits()))
    turned = [1, 0] + forth[2:]

    def weight_grad(a, b, level, name):
        wide_rows, n = a[0].shape[1], b[0].shape[1]
        chunk = wide_rows // size
        half = ((size // 2, chunk, n), BF)
        return local_call(
            functools.partial(weight_body, level),
            [half, half],
            [info] + a + b,
            [pltpu.VMEM((size, chunk, n), BF)],
            name=name,
        )

    second_s, act_s, gate_s, back_s, gsum_s, csum_s = mlp((1, 3), False)
    second_k, act_k, gate_k, back_k, gsum_k, csum_k, resid_own = mlp((0, 2), True)
    beside, far = scatter_near(back_k, back_s)
    cots = [cot_near[b] for b in (1, 3, 0, 2)]
    down_kept, down_sent = weight_grad(cots, [act_s, act_k], 0, "down_grad")
    down_got = swap(down_sent, "rep", 1)
    up_kept, up_sent = weight_grad([second_s, second_k], [gate_s, gate_k], 1, "up_grad")
    up_got = swap(up_sent, "rep", 2)
    grad_mid, mid_low, mid_sums = local_call(
        norm_two_back_body,
        [((block, width), F32), ((block, width), BF), ((3, width), F32)],
        [info, back_k, beside, after(far, down_kept, up_kept), resid_own, cot_near[0], vecs],
        name="norm_two_back",
    )
    mid_near = gather_near(mid_low)
    fwd_s, fwd_k = local_call(
        forward_body,
        [((2 * block, width), BF), ((2 * block, width), F32)],
        [info, after(act_s, mid_low), act_k, w_down],
        name="forward",
    )
    mid_near = list(lax.optimization_barrier(tuple(mid_near) + (fwd_s,)))
    fwd_s = mid_near.pop()
    fwd_beside, fwd_far = scatter_near(fwd_k, fwd_s)

    gs, grad_v, v_sum, *v_pieces = local_call(
        value_back_body,
        [head_shape, ((rows, cols), BF), ((1, cols), F32)] + [((cols, cols), BF)] * group,
        [info] + mid_near + [w_out, probs, first],
        [
            pltpu.VMEM((rows, width), BF),
            pltpu.VMEM((heads, rows, dim), F32),
            pltpu.VMEM((cols, width), BF),
            pltpu.VMEM((group, cols, cols), BF),
        ],
        name="value_back",
    )

    def exchange(pieces):
        return [pieces[0]] + [swap(pieces[r], "grp", r) for r in range(1, group)]

    v_got = exchange(v_pieces)
    grad_q, grad_k, q_sum = local_call(
        query_back_body,
        [((rows, cols), BF), ((rows, cols), BF), ((1, cols), F32)],
        [info, gs, vs, ks, qs, probs],
        [pltpu.VMEM((heads, rows, dim), F32)] * 2,
        name="query_back",
    )
    qk_pieces = local_call(
        pieces_body,
        [((half, width), BF)] * group,
        [info, grad_q, grad_k, first],
        [pltpu.VMEM((cols, width), BF), pltpu.VMEM((group, half, width), BF)],
        name="qk_pieces",
    )
    qk_got = exchange(qk_pieces)
    first_k, first_s, one_sums = local_call(
        first_back_body,
        [((2 * block, width), F32), ((2 * block, width), BF), ((2, width), F32)],
        [info, after(grad_q, qk_pieces[0]), grad_k, grad_v, wq] + x_near,
        name="first_back",
    )
    first_beside, first_far = scatter_near(first_k, first_s)
    (out_full,) = local_call(
        out_grad_body,
        [((width, cols), BF)],
        [info] + mid_near + [after(mixed, first_s)],
        name="out_grad",
    )
    sub = width // size
    top = sub // 32 * 16
    halves = [((size // 2, top, width), BF)] * 2 + [((size // 2, sub - top, width), BF)] * 2
    a_kept, a_sent, b_kept, b_sent = local_call(
        assemble_body,
        halves,
        [info] + v_got + qk_got + [out_full],
        [pltpu.VMEM((3 * width, cols), BF), pltpu.VMEM((size, top, width), BF)]
        + [pltpu.VMEM((size, sub - top, width), BF)],
        name="assemble",
    )
    a_got, b_got = swap(a_sent, "rep", 1), swap(b_sent, "rep", 2)
    (grad_rows,) = local_call(
        norm_one_back_body,
        [((block, width), BF)],
        [info, first_k, first_beside, first_far, x_near[0], grad_mid, vecs],
        name="norm_one_back",
    )

    block_rows = resid_own + (fwd_k[:block] + wide(fwd_beside[:block]) + wide(fwd_far) + vecs[5])

    down_kept, down_got = halve_rest(after(down_kept, mid_near[3]), down_got, forth)
    down_grad = wide(down_kept) + wide(down_got)
    up_kept, up_got = halve_rest(after(up_kept, mid_near[3]), up_got, turned)
    up_grad = wide(up_kept) + wide(up_got)
    qkv_grad, out_grad = local_call(
        finish_body,
        [((cols, 3 * sub), F32), ((sub, cols), F32)],
        [info, *halve_rest(a_kept, a_got, forth), *halve_rest(b_kept, b_got, turned)],
        name="finish",
    )

    vec_kept, vec_sent = local_call(
        vectors_body,
        [((2, 8, cols), F32)] * 2,
        [info, one_sums, mid_sums, q_sum, v_sum, csum_s, csum_k],
        [pltpu.VMEM((group, 8, cols), F32)],
        name="vectors",
    )
    pair = vec_kept + swap(vec_sent, "grp", 1)
    mine = pair[0] + swap(pair[1], "grp", 2)
    up_bias = jnp.pad(gsum_s + gsum_k, ((0, 0), (0, -hidden % cols))).reshape(-1, cols)
    mine = jnp.concatenate([mine, up_bias])
    for level in range(rep_bits()):
        mine = mine + swap(mine, "rep", 1 << level)
    return (
        low(block_rows).reshape(block_input.shape),
        grad_rows.reshape(block_input.shape),
        mine[0],
        mine[1],
        qkv_grad,
        mine[5:7].reshape(-1),
        out_grad.T,
        mine[2],
        mine[3],
        mine[4],
        up_grad,
        mine[8:].reshape(-1)[:hidden],
        down_grad.T,
        mine[7],
    )


def solution(mesh):
    in_specs = (
        P("rep", "grp", None),
        P("rep"),
        P("grp"),
        P("grp"),
        P("grp", None),
        P("grp"),
        P("grp", None),
        P("grp"),
        P("grp"),
        P("grp"),
        P(None, "grp"),
        P("grp"),
        P("grp", None),
        P("grp"),
        P("rep", "grp", None),
    )
    out_specs = (
        P("rep", "grp", None),
        P("rep", "grp", None),
        P("grp"),
        P("grp"),
        P("grp", "rep"),
        P("grp"),
        P("grp", "rep"),
        P("grp"),
        P("grp"),
        P("grp"),
        P("rep", "grp"),
        P("grp"),
        P("grp", "rep"),
        P("grp"),
    )
    return jax.shard_map(
        on_device, mesh=mesh, in_specs=in_specs, out_specs=out_specs, check_vma=False
    )
```

```python
import functools
import math

import jax
import jax.numpy as jnp
from jax import lax
from jax.experimental import pallas as pl
from jax.experimental.pallas import tpu as pltpu
from jax.sharding import PartitionSpec as P

HEADS = 16


EPSILON = 1e-06
GELU_SCALE = 0.7978845608028654
GELU_CUBIC = 0.044715
NEG_FILL = -1000000000.0
BF = jnp.bfloat16
F32 = jnp.float32


def norm_stats(values):
    center = values - jnp.mean(values, axis=-1, keepdims=True)
    inv_std = lax.rsqrt(jnp.mean(center * center, axis=-1, keepdims=True) + EPSILON)
    return center * inv_std, inv_std


def norm_backward(upstream, normed, inv_std, gain):
    scaled = upstream * gain
    return inv_std * (
        scaled
        - jnp.mean(scaled, axis=-1, keepdims=True)
        - normed * jnp.mean(scaled * normed, axis=-1, keepdims=True)
    )


def gelu_with_slope(values):
    square = values * values
    tangent = jnp.tanh(GELU_SCALE * (values + GELU_CUBIC * (values * square)))
    half = 0.5 * (1.0 + tangent)
    slope = half + 0.5 * values * (1.0 - tangent * tangent) * GELU_SCALE * (
        1.0 + 3.0 * GELU_CUBIC * square
    )
    return (values * half, slope)


def low(values):
    return values.astype(BF)


def wide(values):
    return values.astype(F32)


def dot(a, b, dims):
    return lax.dot_general(a, b, (dims, ((), ())), preferred_element_type=F32)


NN = ((1,), (0,))
NT = ((1,), (1,))
TN = ((0,), (0,))


def xor_perm(size, bit):
    return [(i, i ^ bit) for i in range(size)]


def swap(values, axis, bit):
    return lax.ppermute(values, axis, xor_perm(lax.axis_size(axis), bit))


def gather_near(own):
    across = swap(own, "grp", 2)
    beside = swap(own, "grp", 1)
    return [own, beside, across, swap(across, "grp", 1)]


def local_call(body, outs, args, scratch=(), name=None, cost=1000):
    specs = [pl.BlockSpec(memory_space=pltpu.SMEM)]
    specs += [pl.BlockSpec(memory_space=pltpu.VMEM)] * (len(args) - 1)
    return pl.pallas_call(
        body,
        out_shape=[jax.ShapeDtypeStruct(shape, dtype) for shape, dtype in outs],
        in_specs=specs,
        out_specs=[pl.BlockSpec(memory_space=pltpu.VMEM)] * len(outs),
        scratch_shapes=list(scratch),
        compiler_params=pltpu.CompilerParams(vmem_limit_bytes=60000 * 1024),
        cost_estimate=pl.CostEstimate(flops=cost, transcendentals=0, bytes_accessed=cost),
        name=name,
    )(*args)


def unpack_body(info, p0, p1, p2, p3, vecs, bias, spread):
    me = info[0]
    cols = p0.shape[1]
    for r, piece in enumerate((p0, p1, p2, p3)):
        spread[me ^ r] = piece[...]
    for d in range(4):
        vecs[:, d * cols : (d + 1) * cols] = spread[d]
    odd = (me & 1) == 1
    for i in range(2):
        block = spread[2 * i + (me >> 1)]
        bias[i : i + 1, :] = jnp.where(odd, block[7:8, :], block[6:7, :])


def split_w_body(info, w, own, beside, far, flat):
    me, bit = info[0], info[2] & 1
    cols = flat.shape[1]
    half = cols // 2
    width = 4 * cols
    for d in range(4):
        parts = [w[:, j * width + d * cols : j * width + (d + 1) * cols] for j in range(3)]
        flat[me ^ d] = jnp.concatenate(parts, axis=1)
    start = pl.multiple_of(bit * half, 16)
    own[...] = flat[0]
    beside[:cols, :] = flat[1]
    beside[cols:, :] = flat[3, pl.ds(start, half), :]
    far[...] = flat[2, pl.ds(start, half), :]


def norm_one_body(info, x0, x1, x2, x3, vecs, first):
    block = x0.shape[0]
    step = 64
    for r, x in enumerate((x0, x1, x2, x3)):

        def rows(c, carry):
            start = pl.multiple_of(c * step, step)
            normed, _ = norm_stats(wide(x[pl.ds(start, step), :]))
            first[pl.ds(r * block + start, step), :] = low(normed * vecs[0:1, :] + vecs[1:2, :])
            return carry

        lax.fori_loop(0, block // step, rows, 0)


def attend_body(info, first, w0, w1, w2, w3, bias, wq, qs, ks, vs, probs, mixed, ms):
    bit = info[2] & 1
    me, length = info[0], info[1]
    cols = w0.shape[0]
    rows = first.shape[0]
    heads, _, dim = qs.shape
    half = cols // 2
    wq[pl.ds(pl.multiple_of(me * cols, 16), cols), :] = w0[...]
    wq[pl.ds(pl.multiple_of((me ^ 1) * cols, 16), cols), :] = w1[:cols, :]
    for w, side in ((w2, bit), (w3, 1 - bit)):
        for r in (2, 3):
            start = pl.multiple_of((me ^ r) * cols + side * half, 16)
            wq[pl.ds(start, half), :] = w[(r - 2) * half : (r - 1) * half, :]
    for j, (out, shift) in enumerate(((qs, 0), (ks, None), (vs, 1))):
        part = dot(first[...], wq[:, j * cols : (j + 1) * cols], NN)
        if shift is not None:
            part = part + bias[shift : shift + 1, :]
        part = low(part)
        for h in range(heads):
            out[h] = part[:, h * dim : (h + 1) * dim]
    block = rows // 4
    spot = lax.broadcasted_iota(jnp.int32, (1, rows), 1)
    near = spot // block
    live = ((me ^ near) * block + (spot - near * block)) < length
    scale = 1.0 / math.sqrt(dim)
    step = 256

    def one(i, carry):
        h = i // (rows // step)
        start = pl.multiple_of((i % (rows // step)) * step, step)
        scores = dot(qs[h, pl.ds(start, step), :], ks[h], NT) * scale
        scores = jnp.where(live, scores, NEG_FILL)
        top = jnp.max(scores, axis=-1, keepdims=True)
        raised = jnp.exp(scores - top)
        share = low(raised * (1.0 / jnp.sum(raised, axis=-1, keepdims=True)))
        probs[h, pl.ds(start, step), :] = share
        ms[h, pl.ds(start, step), :] = low(dot(share, vs[h], NN))
        return carry

    lax.fori_loop(0, heads * (rows // step), one, 0, unroll=2)
    for t in range(4):
        parts = [ms[h, t * block : (t + 1) * block, :] for h in range(heads)]
        mixed[:, t * cols : (t + 1) * cols] = jnp.concatenate(parts, axis=1)


def mlp_body(
    blocks, keep, info, m0, m1, m2, m3, o0, o1, o2, o2b, o3, o3b, xa, xb, ca, cb, vecs, w_up, b_up, w_down,
    second, activated, gate_low, back, gate_sum, cot_sum, *rest
):
    w_far = rest[-1]
    block = xa.shape[0]
    cols = o0.shape[0]
    half = cols // 2
    bit = info[2] & 1
    for i, (w, side) in enumerate(((o2, bit), (o2b, 1 - bit), (o3, bit), (o3b, 1 - bit))):
        start = pl.multiple_of((i // 2) * cols + side * half, 16)
        w_far[pl.ds(start, half), :] = w[...]
    total = None
    for r, m in enumerate((m0, m1, m2, m3)):
        lhs = jnp.concatenate(
            [m[:, (b ^ r) * cols : ((b ^ r) + 1) * cols] for b in blocks], axis=0
        )
        if r < 2:
            w = (o0, o1)[r][...]
        else:
            w = w_far[(r - 2) * cols : (r - 1) * cols, :]
        term = dot(lhs, w, NN)
        total = term if total is None else total + term
    resid = jnp.concatenate([wide(xa[...]), wide(xb[...])], axis=0) + (total + vecs[2:3, :])
    normed, _ = norm_stats(resid)
    second[...] = low(normed * vecs[3:4, :] + vecs[4:5, :])
    if keep:
        rest[0][...] = resid[:block, :]
    cot = jnp.concatenate([ca[...], cb[...]], axis=0)
    cot_sum[...] = jnp.sum(wide(cot), axis=0, keepdims=True)
    act, slope = gelu_with_slope(dot(second[...], w_up[...], NT) + wide(b_up[...]))
    activated[...] = low(act)
    gate = dot(cot, w_down[...], NT) * slope
    gate_sum[...] = jnp.sum(gate, axis=0, keepdims=True)
    gate_low[...] = low(gate)
    back[...] = dot(gate_low[...], w_up[...], NN).astype(back.dtype)


def forward_body(info, act_s, act_k, w_down, sent, kept):
    sent[...] = low(dot(act_s[...], w_down[...], NN))
    kept[...] = dot(act_k[...], w_down[...], NN)


def chunk_index(i, level, bit):
    return ((i >> level) << (level + 1)) | (bit << level) | (i & ((1 << level) - 1))


def split_halves(chunks, kept, sent, level, position):
    mine = (position >> level) & 1
    second = chunks.shape[0] // 4
    for i in range(kept.shape[0]):
        for out, bit in ((kept, mine), (sent, 1 - mine)):
            label = chunk_index(i, level, bit)
            out[i] = chunks[label ^ ((label >> 1) & second)]


def weight_body(level, info, *refs):
    kept, sent, chunks = refs[-3:]
    a = [r[...] for r in refs[: len(refs) - 3] if r.shape[1] == refs[0].shape[1]]
    b = [r[...] for r in refs[: len(refs) - 3] if r.shape[1] != refs[0].shape[1]]
    full = low(dot(jnp.concatenate(a, axis=0), jnp.concatenate(b, axis=0), TN))
    size, rows, _ = chunks.shape
    for c in range(size):
        chunks[c] = full[c * rows : (c + 1) * rows, :]
    split_halves(chunks, kept, sent, level, info[3])


def out_grad_body(info, g0, g1, g2, g3, mixed, out):
    cols = out.shape[1]
    a = jnp.concatenate([g0[...], g1[...], g2[...], g3[...]], axis=0)
    b = jnp.concatenate([mixed[:, t * cols : (t + 1) * cols] for t in range(4)], axis=0)
    out[...] = low(dot(a, b, TN))


def assemble_body(info, *refs):
    me = info[0]
    v, qk, out_full = refs[0:4], refs[4:8], refs[8]
    kept_a, sent_a, kept_b, sent_b, flat, part_a, part_b = refs[9:]
    cols = flat.shape[1]
    half = cols // 2
    width = 4 * cols
    for r in range(4):
        for t in range(4):
            start = pl.multiple_of((t // 2) * width + (me ^ r) * cols + (t % 2) * half, 16)
            flat[pl.ds(start, half), :] = qk[r][:, t * cols : (t + 1) * cols]
        flat[pl.ds(pl.multiple_of(2 * width + (me ^ r) * cols, 16), cols), :] = v[r][...]
    size, top, _ = part_a.shape
    sub = top + part_b.shape[1]
    for c in range(size):
        for b in range(4):
            lanes = slice(b * cols, (b + 1) * cols)
            source, start = (out_full, c * sub) if b == 3 else (flat, (3 * c + b) * sub)
            part_a[c, :, lanes] = source[start : start + top, :]
            part_b[c, :, lanes] = source[start + top : start + sub, :]
    split_halves(part_a, kept_a, sent_a, 0, info[3])
    split_halves(part_b, kept_b, sent_b, 1, info[3])


def finish_body(info, kept_a, got_a, kept_b, got_b, qkv, out):
    total = jnp.concatenate(
        [wide(kept_a[...]) + wide(got_a[...]), wide(kept_b[...]) + wide(got_b[...])], axis=0
    )
    cols = out.shape[1]
    turned = [total[:, b * cols : (b + 1) * cols].T for b in range(3)]
    qkv[...] = jnp.concatenate(turned, axis=1)
    out[...] = total[:, 3 * cols :]


def vectors_body(info, one, mid, q_sum, v_sum, cot_a, cot_b, kept, sent, spread):
    me = info[0]
    cols = q_sum.shape[1]
    cot = 0.25 * (cot_a[...] + cot_b[...])
    spread[...] = jnp.zeros_like(spread)
    for d in range(4):
        lanes = slice(d * cols, (d + 1) * cols)
        spread[d, 0:2, :] = one[:, lanes]
        spread[d, 2:5, :] = mid[:, lanes]
        spread[d, 7:8, :] = cot[:, lanes]
    row = lax.broadcasted_iota(jnp.int32, (2, cols), 0)
    spread[me >> 1, 5:7, :] = jnp.where(row == (me & 1), q_sum[...], 0.0)
    spread[2 + (me >> 1), 5:7, :] = jnp.where(row == (me & 1), v_sum[...], 0.0)
    for i in range(2):
        kept[i] = spread[me ^ (2 * i)]
        sent[i] = spread[me ^ (2 * i + 1)]


def norm_two_back_body(info, kept, beside, far, resid, cot, vecs, grad_mid, mid_low, sums):
    block = resid.shape[0]
    grad_second = kept[:block, :] + wide(beside[:block, :]) + wide(far[...])
    normed, inv = norm_stats(resid[...])
    grad = wide(cot[...]) + norm_backward(grad_second, normed, inv, vecs[3:4, :])
    grad_mid[...] = grad
    mid_low[...] = low(grad)
    sums[0:1, :] = jnp.sum(grad, axis=0, keepdims=True)
    sums[1:2, :] = jnp.sum(grad_second * normed, axis=0, keepdims=True)
    sums[2:3, :] = jnp.sum(grad_second, axis=0, keepdims=True)


def value_back_body(
    info, g0, g1, g2, g3, w_out, probs, first, gs, grad_v, v_sum, o0, o1, o2, o3, mid, vacc, flat, pieces
):
    me = info[0]
    block = g0.shape[0]
    heads, rows, dim = gs.shape
    cols = heads * dim
    for r, g in enumerate((g0, g1, g2, g3)):
        mid[r * block : (r + 1) * block, :] = g[...]
    grad_mixed = low(dot(mid[...], w_out[...], NT))
    for h in range(heads):
        gs[h] = grad_mixed[:, h * dim : (h + 1) * dim]

    def one(h, carry):
        vacc[h] = dot(probs[h], gs[h], TN)
        return carry

    lax.fori_loop(0, heads, one, 0)
    grad = jnp.concatenate([vacc[h] for h in range(heads)], axis=1)
    v_sum[...] = jnp.sum(grad, axis=0, keepdims=True)
    grad_v[...] = low(grad)
    flat[...] = low(dot(grad_v[...], first[...], TN))
    for d in range(4):
        pieces[me ^ d] = flat[:, d * cols : (d + 1) * cols]
    for r, out in enumerate((o0, o1, o2, o3)):
        out[...] = pieces[r]


def query_back_body(info, gs, vs, ks, qs, probs, grad_q, grad_k, q_sum, qacc, kacc):
    heads, rows, dim = gs.shape
    scale = 1.0 / math.sqrt(dim)
    step = 256
    kacc[...] = jnp.zeros_like(kacc)

    def one(i, carry):
        h = i // (rows // step)
        start = pl.multiple_of((i % (rows // step)) * step, step)
        here = pl.ds(start, step)
        g = gs[h, here, :]
        share = wide(probs[h, here, :])
        dprob = dot(g, vs[h], NT)
        delta = jnp.sum(share * dprob, axis=-1, keepdims=True)
        dscore = low(share * (dprob - delta) * scale)
        qacc[h, here, :] = dot(dscore, ks[h], NN)
        kacc[h] += dot(dscore, qs[h, here, :], TN)
        return carry

    lax.fori_loop(0, heads * (rows // step), one, 0, unroll=2)
    grad = jnp.concatenate([qacc[h] for h in range(heads)], axis=1)
    q_sum[...] = jnp.sum(grad, axis=0, keepdims=True)
    grad_q[...] = low(grad)
    grad_k[...] = low(jnp.concatenate([kacc[h] for h in range(heads)], axis=1))


def pieces_body(info, grad_a, grad_b, first, o0, o1, o2, o3, flat, pieces):
    me = info[0]
    cols = grad_a.shape[1]
    half = cols // 2
    for j, grad in enumerate((grad_a, grad_b)):
        flat[...] = low(dot(grad[...], first[...], TN))
        for d in range(4):
            for t in range(2):
                pieces[me ^ d, :, (2 * j + t) * cols : (2 * j + t + 1) * cols] = flat[
                    t * half : (t + 1) * half, d * cols : (d + 1) * cols
                ]
    for r, out in enumerate((o0, o1, o2, o3)):
        out[...] = pieces[r]


def first_back_body(info, grad_q, grad_k, grad_v, wq, x0, x1, x2, x3, kept, sent, sums):
    cols = grad_q.shape[1]
    block = x0.shape[0]
    total = None
    for j, grad in enumerate((grad_q, grad_k, grad_v)):
        term = dot(grad[...], wq[:, j * cols : (j + 1) * cols], NT)
        total = term if total is None else total + term
    gain = shift = 0.0
    for r, x in enumerate((x0, x1, x2, x3)):
        part = total[r * block : (r + 1) * block, :]
        normed, _ = norm_stats(wide(x[...]))
        gain = gain + jnp.sum(part * normed, axis=0, keepdims=True)
        shift = shift + jnp.sum(part, axis=0, keepdims=True)
        place = slice((r // 2) * block, (r // 2 + 1) * block)
        if r % 2:
            sent[place, :] = low(part)
        else:
            kept[place, :] = part
    sums[0:1, :] = gain
    sums[1:2, :] = shift


def norm_one_back_body(info, kept, beside, far, x, grad_mid, vecs, out):
    block = x.shape[0]
    normed, inv = norm_stats(wide(x[...]))
    grad_first = kept[:block, :] + wide(beside[:block, :]) + wide(far[...])
    out[...] = low(grad_mid[...] + norm_backward(grad_first, normed, inv, vecs[0:1, :]))


def scatter_near(kept, sent, *others):
    block = kept.shape[0] // 2
    beside = swap(sent, "grp", 1)
    far = low(kept[block:] + wide(beside[block:]))
    return beside, swap(after(far, *others) if others else far, "grp", 2)


def after(values, *others):
    return lax.optimization_barrier((values,) + others)[0]


def rep_bits():
    return lax.axis_size("rep").bit_length() - 1


def rep_label():
    position = lax.axis_index("rep")
    return position ^ ((position >> 1) & (1 << (rep_bits() - 2)))


def rep_swap(values, level):
    top = rep_bits() - 1
    return swap(values, "rep", (3 << (top - 1)) if level == top else (1 << level))


def halve_open(kept, got, order):
    left = sorted(order)
    left.remove(order[0])
    shape = (2,) * len(left) + kept.shape[1:]
    return kept.reshape(shape), got.reshape(shape), left, list(order[1:])


def halve_next(state):
    kept, got, left, order = state
    if not order:
        return state
    level = order[0]
    mine = (rep_label() >> level) & 1
    axis = len(left) - 1 - left.index(level)

    def pick(values, bit):
        return wide(lax.dynamic_index_in_dim(values, bit, axis, keepdims=False))

    got_next = rep_swap(low(pick(kept, 1 - mine) + pick(got, 1 - mine)), level)
    kept = pick(kept, mine) + pick(got, mine)
    return kept, got_next, [x for x in left if x != level], order[1:]


def halve_after(state, *others):
    return (state[0], after(state[1], *others)) + state[2:]


def halve_rest(state):
    while state[3]:
        state = halve_next(state)
    return state[0], state[1]


def on_device(
    block_input,
    lengths,
    ln1_gain,
    ln1_bias,
    w_qkv,
    b_qv,
    w_out,
    b_out,
    ln2_gain,
    ln2_bias,
    w_up,
    b_up,
    w_down,
    b_down,
    cotangent,
):
    images, block, width = block_input.shape
    group = lax.axis_size("grp")
    assert images == 1 and group == 4
    me = lax.axis_index("grp")
    order = me ^ jnp.arange(group)
    cols = width // group
    heads = HEADS // group
    dim = width // HEADS
    rows = group * block
    hidden = w_up.shape[1]
    info = jnp.stack(
        [me.astype(jnp.int32), lengths[0], lax.axis_index("rep").astype(jnp.int32)]
        + [rep_label().astype(jnp.int32)]
    )

    x_near = gather_near(block_input.reshape(block, width))
    half = cols // 2
    w_own, w_beside, w_far = local_call(
        split_w_body,
        [((cols, 3 * cols), BF), ((cols + half, 3 * cols), BF), ((half, 3 * cols), BF)],
        [info, after(w_qkv, x_near[1])],
        [pltpu.VMEM((group, cols, 3 * cols), BF)],
        name="split_w",
        cost=40_000_000,
    )
    small = [after(ln1_gain, w_own), ln1_bias, b_out, ln2_gain, ln2_bias, b_down]
    packed = jnp.concatenate([wide(v) for v in small] + [wide(b_qv)]).reshape(8, cols)
    packed_near = gather_near(packed)
    w_beside = swap(w_beside, "grp", 1)
    w_across = swap(
        after(jnp.concatenate([w_far, w_beside[cols:]]), x_near[2], packed_near[2]), "grp", 2
    )
    vecs, qv_bias = local_call(
        unpack_body,
        [((8, width), F32), ((2, cols), F32)],
        [info] + packed_near,
        [pltpu.VMEM((group, 8, cols), F32)],
        name="unpack",
    )
    cot_near = gather_near(cotangent.reshape(block, width))
    side = lax.axis_index("rep") & 1
    out_half = swap(lax.dynamic_slice_in_dim(w_out, side * half, half, 0), "grp", 2)
    out_other = swap(out_half, "rep", 1)
    out_near = [w_out, swap(w_out, "grp", 1), out_half, out_other]
    out_near += [swap(out_half, "grp", 1), swap(out_other, "grp", 1)]

    (first,) = local_call(
        norm_one_body, [((rows, width), BF)], [info] + x_near + [vecs], name="norm_one"
    )
    w_across, first = lax.optimization_barrier((w_across, first))
    w_near = [w_own, w_beside, w_across, swap(w_across, "rep", 1)]
    head_shape = ((heads, rows, dim), BF)
    wq, qs, ks, vs, probs, mixed = local_call(
        attend_body,
        [((width, 3 * cols), BF), head_shape, head_shape, head_shape]
        + [((heads, rows, rows), BF), ((block, width), BF)],
        [info, first] + w_near + [qv_bias],
        [pltpu.VMEM((heads, rows, dim), BF)],
        name="attend",
    )

    mixed_near = gather_near(mixed)

    def mlp(blocks, keep):
        kind = F32 if keep else BF
        outs = [((2 * block, width), BF), ((2 * block, hidden), BF), ((2 * block, hidden), BF)]
        outs += [((2 * block, width), kind)]
        outs += [((1, hidden), F32), ((1, width), F32)]
        if keep:
            outs += [((block, width), F32)]
        args = [info] + mixed_near + out_near + [x_near[b] for b in blocks]
        args += [cot_near[b] for b in blocks] + [vecs, w_up.T, b_up.reshape(1, -1), w_down]
        return local_call(
            functools.partial(mlp_body, blocks, keep),
            outs,
            args,
            [pltpu.VMEM((2 * cols, width), BF)],
            name="mlp",
        )

    size = lax.axis_size("rep")
    forth = list(range(rep_bits()))
    turned = [1, 0] + forth[2:]
    inner = [1, forth[-1], 0] + forth[2:-1]

    def weight_grad(a, b, level, name):
        wide_rows, n = a[0].shape[1], b[0].shape[1]
        chunk = wide_rows // size
        half = ((size // 2, chunk, n), BF)
        return local_call(
            functools.partial(weight_body, level),
            [half, half],
            [info] + a + b,
            [pltpu.VMEM((size, chunk, n), BF)],
            name=name,
        )

    second_s, act_s, gate_s, back_s, gsum_s, csum_s = mlp((1, 3), False)
    second_k, act_k, gate_k, back_k, gsum_k, csum_k, resid_own = mlp((0, 2), True)
    beside, far = scatter_near(back_k, back_s)
    cots = [cot_near[b] for b in (1, 3, 0, 2)]
    down_kept, down_sent = weight_grad(cots, [act_s, act_k], 0, "down_grad")
    down_got = swap(down_sent, "rep", 1)
    up_kept, up_sent = weight_grad([second_s, second_k], [gate_s, gate_k], 1, "up_grad")
    up_got = swap(up_sent, "rep", 2)
    grad_mid, mid_low, mid_sums = local_call(
        norm_two_back_body,
        [((block, width), F32), ((block, width), BF), ((3, width), F32)],
        [info, back_k, beside, after(far, down_kept, up_kept), resid_own, cot_near[0], vecs],
        name="norm_two_back",
    )
    mid_across = swap(mid_low, "grp", 2)
    fwd_s, fwd_k = local_call(
        forward_body,
        [((2 * block, width), BF), ((2 * block, width), F32)],
        [info, after(act_s, mid_low), act_k, w_down],
        name="forward",
    )
    mid_across, fwd_s = lax.optimization_barrier((mid_across, fwd_s))
    mid_near = [mid_low, swap(mid_low, "grp", 1), mid_across, swap(mid_across, "grp", 1)]

    gs, grad_v, v_sum, *v_pieces = local_call(
        value_back_body,
        [head_shape, ((rows, cols), BF), ((1, cols), F32)] + [((cols, cols), BF)] * group,
        [info] + mid_near + [w_out, probs, first],
        [
            pltpu.VMEM((rows, width), BF),
            pltpu.VMEM((heads, rows, dim), F32),
            pltpu.VMEM((cols, width), BF),
            pltpu.VMEM((group, cols, cols), BF),
        ],
        name="value_back",
    )

    down_state = halve_open(down_kept, down_got, forth)
    up_state = halve_open(up_kept, up_got, inner)
    gs, down_now, up_now = lax.optimization_barrier((gs, down_state[1], up_state[1]))
    down_state = halve_next((down_state[0], down_now) + down_state[2:])
    up_state = halve_next((up_state[0], up_now) + up_state[2:])

    def exchange(pieces):
        return [pieces[0]] + [swap(pieces[r], "grp", r) for r in range(1, group)]

    v_got = exchange(v_pieces)
    grad_q, grad_k, q_sum = local_call(
        query_back_body,
        [((rows, cols), BF), ((rows, cols), BF), ((1, cols), F32)],
        [info, gs, vs, ks, qs, probs],
        [pltpu.VMEM((heads, rows, dim), F32)] * 2,
        name="query_back",
    )
    up_now = up_state[1]
    grad_k, down_now, *v_got = lax.optimization_barrier((grad_k, down_state[1], *v_got))
    qk_pieces = local_call(
        pieces_body,
        [((half, width), BF)] * group,
        [info, grad_q, grad_k, first],
        [pltpu.VMEM((cols, width), BF), pltpu.VMEM((group, half, width), BF)],
        name="qk_pieces",
    )
    qk_got = exchange(qk_pieces)
    down_now, up_now, _ = lax.optimization_barrier((down_now, up_now, qk_pieces[0]))
    down_state = halve_next((down_state[0], down_now) + down_state[2:])
    up_state = halve_next((up_state[0], up_now) + up_state[2:])
    first_k, first_s, one_sums = local_call(
        first_back_body,
        [((2 * block, width), F32), ((2 * block, width), BF), ((2, width), F32)],
        [info, after(grad_q, qk_pieces[0], down_state[0], up_state[0]), grad_k, grad_v, wq] + x_near,
        name="first_back",
    )
    vec_kept, vec_sent = local_call(
        vectors_body,
        [((2, 8, cols), F32)] * 2,
        [info, one_sums, mid_sums, q_sum, v_sum, csum_s, csum_k],
        [pltpu.VMEM((group, 8, cols), F32)],
        name="vectors",
    )
    (out_full,) = local_call(
        out_grad_body,
        [((width, cols), BF)],
        [info] + mid_near + [after(mixed, first_s, vec_sent)],
        name="out_grad",
    )
    down_now, up_now, out_full = lax.optimization_barrier((down_state[1], up_state[1], out_full))
    down_state = (down_state[0], down_now) + down_state[2:]
    up_state = (up_state[0], up_now) + up_state[2:]
    sub = width // size
    top = sub // 32 * 16
    halves = [((size // 2, top, width), BF)] * 2 + [((size // 2, sub - top, width), BF)] * 2
    a_kept, a_sent, b_kept, b_sent = local_call(
        assemble_body,
        halves,
        [info] + v_got + qk_got + [out_full],
        [pltpu.VMEM((3 * width, cols), BF), pltpu.VMEM((size, top, width), BF)]
        + [pltpu.VMEM((size, sub - top, width), BF)],
        name="assemble",
    )
    a_state = halve_open(a_kept, swap(a_sent, "rep", 1), forth)
    b_state = halve_open(b_kept, swap(b_sent, "rep", 2), turned)
    first_beside, first_far = scatter_near(first_k, after(first_s, a_sent, b_sent))
    pair = vec_kept + swap(after(vec_sent, a_sent, b_sent), "grp", 1)
    fwd_beside, fwd_far = scatter_near(fwd_k, after(fwd_s, a_sent, b_sent))
    mine = pair[0] + swap(pair[1], "grp", 2)
    up_bias = jnp.pad(gsum_s + gsum_k, ((0, 0), (0, -hidden % cols))).reshape(-1, cols)
    mine = jnp.concatenate([mine, up_bias])
    for level in range(rep_bits()):
        mine_got, a_now, b_now, first_far = lax.optimization_barrier(
            (rep_swap(mine, level), a_state[1], b_state[1], first_far)
        )
        a_state = halve_next((a_state[0], a_now) + a_state[2:])
        b_state = halve_next((b_state[0], b_now) + b_state[2:])
        mine = mine + mine_got
        if level == 0:
            down_state = halve_after(down_state, a_now)
            up_state = halve_after(up_state, a_now)
            (grad_rows,) = local_call(
                norm_one_back_body,
                [((block, width), BF)],
                [info, first_k, first_beside, first_far, x_near[0], grad_mid, vecs],
                name="norm_one_back",
            )
    block_rows = resid_own + (fwd_k[:block] + wide(fwd_beside[:block]) + wide(fwd_far) + vecs[5])
    down_kept, down_got = halve_rest(down_state)
    down_grad = wide(down_kept) + wide(down_got)
    up_kept, up_got = halve_rest(up_state)
    up_grad = wide(up_kept) + wide(up_got)
    qkv_grad, out_grad = local_call(
        finish_body,
        [((cols, 3 * sub), F32), ((sub, cols), F32)],
        [info, *halve_rest(a_state), *halve_rest(b_state)],
        name="finish",
    )

    return (
        low(block_rows).reshape(block_input.shape),
        grad_rows.reshape(block_input.shape),
        mine[0],
        mine[1],
        qkv_grad,
        mine[5:7].reshape(-1),
        out_grad.T,
        mine[2],
        mine[3],
        mine[4],
        up_grad,
        mine[8:].reshape(-1)[:hidden],
        down_grad.T,
        mine[7],
    )


def solution(mesh):
    in_specs = (
        P("rep", "grp", None),
        P("rep"),
        P("grp"),
        P("grp"),
        P("grp", None),
        P("grp"),
        P("grp", None),
        P("grp"),
        P("grp"),
        P("grp"),
        P(None, "grp"),
        P("grp"),
        P("grp", None),
        P("grp"),
        P("rep", "grp", None),
    )
    out_specs = (
        P("rep", "grp", None),
        P("rep", "grp", None),
        P("grp"),
        P("grp"),
        P("grp", "rep"),
        P("grp"),
        P("grp", "rep"),
        P("grp"),
        P("grp"),
        P("grp"),
        P("rep", "grp"),
        P("grp"),
        P("grp", "rep"),
        P("grp"),
    )
    return jax.shard_map(
        on_device, mesh=mesh, in_specs=in_specs, out_specs=out_specs, check_vma=False
    )
```

```python
import functools
import math

import jax
import jax.numpy as jnp
from jax import lax
from jax.experimental import pallas as pl
from jax.experimental.pallas import tpu as pltpu
from jax.sharding import PartitionSpec as P

HEADS = 16


EPSILON = 1e-06
GELU_SCALE = 0.7978845608028654
GELU_CUBIC = 0.044715
NEG_FILL = -1000000000.0
BF = jnp.bfloat16
F32 = jnp.float32


def norm_stats(values):
    center = values - jnp.mean(values, axis=-1, keepdims=True)
    inv_std = lax.rsqrt(jnp.mean(center * center, axis=-1, keepdims=True) + EPSILON)
    return center * inv_std, inv_std


def norm_backward(upstream, normed, inv_std, gain):
    scaled = upstream * gain
    return inv_std * (
        scaled
        - jnp.mean(scaled, axis=-1, keepdims=True)
        - normed * jnp.mean(scaled * normed, axis=-1, keepdims=True)
    )


def gelu_with_slope(values):
    square = values * values
    tangent = jnp.tanh(GELU_SCALE * (values + GELU_CUBIC * (values * square)))
    half = 0.5 * (1.0 + tangent)
    slope = half + 0.5 * values * (1.0 - tangent * tangent) * GELU_SCALE * (
        1.0 + 3.0 * GELU_CUBIC * square
    )
    return (values * half, slope)


def low(values):
    return values.astype(BF)


def wide(values):
    return values.astype(F32)


def dot(a, b, dims):
    return lax.dot_general(a, b, (dims, ((), ())), preferred_element_type=F32)


NN = ((1,), (0,))
NT = ((1,), (1,))
TN = ((0,), (0,))


def xor_perm(size, bit):
    return [(i, i ^ bit) for i in range(size)]


def swap(values, axis, bit):
    return lax.ppermute(values, axis, xor_perm(lax.axis_size(axis), bit))


def gather_near(own):
    across = swap(own, "grp", 2)
    beside = swap(own, "grp", 1)
    return [own, beside, across, swap(across, "grp", 1)]


def local_call(body, outs, args, scratch=(), name=None, cost=1000):
    specs = [pl.BlockSpec(memory_space=pltpu.SMEM)]
    specs += [pl.BlockSpec(memory_space=pltpu.VMEM)] * (len(args) - 1)
    return pl.pallas_call(
        body,
        out_shape=[jax.ShapeDtypeStruct(shape, dtype) for shape, dtype in outs],
        in_specs=specs,
        out_specs=[pl.BlockSpec(memory_space=pltpu.VMEM)] * len(outs),
        scratch_shapes=list(scratch),
        compiler_params=pltpu.CompilerParams(vmem_limit_bytes=60000 * 1024),
        cost_estimate=pl.CostEstimate(flops=cost, transcendentals=0, bytes_accessed=cost),
        name=name,
    )(*args)


def unpack_body(info, p0, p1, p2, p3, vecs, bias, spread):
    me = info[0]
    cols = p0.shape[1]
    for r, piece in enumerate((p0, p1, p2, p3)):
        spread[me ^ r] = piece[...]
    for d in range(4):
        vecs[:, d * cols : (d + 1) * cols] = spread[d]
    odd = (me & 1) == 1
    for i in range(2):
        block = spread[2 * i + (me >> 1)]
        bias[i : i + 1, :] = jnp.where(odd, block[7:8, :], block[6:7, :])


def split_w_body(info, w, own, beside, far, flat):
    me, bit = info[0], info[2] & 1
    cols = flat.shape[1]
    half = cols // 2
    width = 4 * cols
    for d in range(4):
        parts = [w[:, j * width + d * cols : j * width + (d + 1) * cols] for j in range(3)]
        flat[me ^ d] = jnp.concatenate(parts, axis=1)
    start = pl.multiple_of(bit * half, 16)
    own[...] = flat[0]
    beside[:cols, :] = flat[1]
    beside[cols:, :] = flat[3, pl.ds(start, half), :]
    far[...] = flat[2, pl.ds(start, half), :]


def norm_one_body(info, x0, x1, x2, x3, vecs, first):
    block = x0.shape[0]
    step = 64
    for r, x in enumerate((x0, x1, x2, x3)):

        def rows(c, carry):
            start = pl.multiple_of(c * step, step)
            normed, _ = norm_stats(wide(x[pl.ds(start, step), :]))
            first[pl.ds(r * block + start, step), :] = low(normed * vecs[0:1, :] + vecs[1:2, :])
            return carry

        lax.fori_loop(0, block // step, rows, 0)


def attend_body(info, first, w0, w1, w2, w3, bias, wq, qs, ks, vs, probs, mixed, ms):
    bit = info[2] & 1
    me, length = info[0], info[1]
    cols = w0.shape[0]
    rows = first.shape[0]
    heads, _, dim = qs.shape
    half = cols // 2
    wq[pl.ds(pl.multiple_of(me * cols, 16), cols), :] = w0[...]
    wq[pl.ds(pl.multiple_of((me ^ 1) * cols, 16), cols), :] = w1[:cols, :]
    for w, side in ((w2, bit), (w3, 1 - bit)):
        for r in (2, 3):
            start = pl.multiple_of((me ^ r) * cols + side * half, 16)
            wq[pl.ds(start, half), :] = w[(r - 2) * half : (r - 1) * half, :]
    for j, (out, shift) in enumerate(((qs, 0), (ks, None), (vs, 1))):
        part = dot(first[...], wq[:, j * cols : (j + 1) * cols], NN)
        if shift is not None:
            part = part + bias[shift : shift + 1, :]
        part = low(part)
        for h in range(heads):
            out[h] = part[:, h * dim : (h + 1) * dim]
    block = rows // 4
    spot = lax.broadcasted_iota(jnp.int32, (1, rows), 1)
    near = spot // block
    live = ((me ^ near) * block + (spot - near * block)) < length
    scale = 1.0 / math.sqrt(dim)
    step = 256

    def one(i, carry):
        h = i // (rows // step)
        start = pl.multiple_of((i % (rows // step)) * step, step)
        scores = dot(qs[h, pl.ds(start, step), :], ks[h], NT) * scale
        scores = jnp.where(live, scores, NEG_FILL)
        top = jnp.max(scores, axis=-1, keepdims=True)
        raised = jnp.exp(scores - top)
        share = low(raised * (1.0 / jnp.sum(raised, axis=-1, keepdims=True)))
        probs[h, pl.ds(start, step), :] = share
        ms[h, pl.ds(start, step), :] = low(dot(share, vs[h], NN))
        return carry

    lax.fori_loop(0, heads * (rows // step), one, 0, unroll=2)
    for t in range(4):
        parts = [ms[h, t * block : (t + 1) * block, :] for h in range(heads)]
        mixed[:, t * cols : (t + 1) * cols] = jnp.concatenate(parts, axis=1)


def mlp_body(
    blocks, keep, info, m0, m1, m2, m3, o0, o1, o2, o2b, o3, o3b, xa, xb, ca, cb, vecs, w_up, b_up, w_down,
    second, activated, gate_low, back, gate_sum, cot_sum, *rest
):
    w_far = rest[-1]
    block = xa.shape[0]
    cols = o0.shape[0]
    half = cols // 2
    bit = info[2] & 1
    for i, (w, side) in enumerate(((o2, bit), (o2b, 1 - bit), (o3, bit), (o3b, 1 - bit))):
        start = pl.multiple_of((i // 2) * cols + side * half, 16)
        w_far[pl.ds(start, half), :] = w[...]
    total = None
    for r, m in enumerate((m0, m1, m2, m3)):
        lhs = jnp.concatenate(
            [m[:, (b ^ r) * cols : ((b ^ r) + 1) * cols] for b in blocks], axis=0
        )
        if r < 2:
            w = (o0, o1)[r][...]
        else:
            w = w_far[(r - 2) * cols : (r - 1) * cols, :]
        term = dot(lhs, w, NN)
        total = term if total is None else total + term
    resid = jnp.concatenate([wide(xa[...]), wide(xb[...])], axis=0) + (total + vecs[2:3, :])
    normed, _ = norm_stats(resid)
    second[...] = low(normed * vecs[3:4, :] + vecs[4:5, :])
    if keep:
        rest[0][...] = resid[:block, :]
    cot = jnp.concatenate([ca[...], cb[...]], axis=0)
    cot_sum[...] = jnp.sum(wide(cot), axis=0, keepdims=True)
    act, slope = gelu_with_slope(dot(second[...], w_up[...], NT) + wide(b_up[...]))
    activated[...] = low(act)
    gate = dot(cot, w_down[...], NT) * slope
    gate_sum[...] = jnp.sum(gate, axis=0, keepdims=True)
    gate_low[...] = low(gate)
    back[...] = dot(gate_low[...], w_up[...], NN).astype(back.dtype)


def forward_body(info, act_s, act_k, w_down, sent, kept):
    sent[...] = low(dot(act_s[...], w_down[...], NN))
    kept[...] = dot(act_k[...], w_down[...], NN)


def chunk_index(i, level, bit):
    return ((i >> level) << (level + 1)) | (bit << level) | (i & ((1 << level) - 1))


def split_halves(chunks, kept, sent, level, position):
    mine = (position >> level) & 1
    second = chunks.shape[0] // 4
    for i in range(kept.shape[0]):
        for out, bit in ((kept, mine), (sent, 1 - mine)):
            label = chunk_index(i, level, bit)
            out[i] = chunks[label ^ ((label >> 1) & second)]


def weight_body(level, info, *refs):
    kept, sent, chunks = refs[-3:]
    a = [r[...] for r in refs[: len(refs) - 3] if r.shape[1] == refs[0].shape[1]]
    b = [r[...] for r in refs[: len(refs) - 3] if r.shape[1] != refs[0].shape[1]]
    full = low(dot(jnp.concatenate(a, axis=0), jnp.concatenate(b, axis=0), TN))
    size, rows, _ = chunks.shape
    for c in range(size):
        chunks[c] = full[c * rows : (c + 1) * rows, :]
    split_halves(chunks, kept, sent, level, info[3])


def out_grad_body(info, g0, g1, g2, g3, mixed, out):
    cols = out.shape[1]
    a = jnp.concatenate([g0[...], g1[...], g2[...], g3[...]], axis=0)
    b = jnp.concatenate([mixed[:, t * cols : (t + 1) * cols] for t in range(4)], axis=0)
    out[...] = low(dot(a, b, TN))


def assemble_body(info, *refs):
    me = info[0]
    v, qk, out_full = refs[0:4], refs[4:8], refs[8]
    kept_a, sent_a, kept_b, sent_b, flat, part_a, part_b = refs[9:]
    cols = flat.shape[1]
    half = cols // 2
    width = 4 * cols
    for r in range(4):
        for t in range(4):
            start = pl.multiple_of((t // 2) * width + (me ^ r) * cols + (t % 2) * half, 16)
            flat[pl.ds(start, half), :] = qk[r][:, t * cols : (t + 1) * cols]
        flat[pl.ds(pl.multiple_of(2 * width + (me ^ r) * cols, 16), cols), :] = v[r][...]
    size, top, _ = part_a.shape
    sub = top + part_b.shape[1]
    for c in range(size):
        for b in range(4):
            lanes = slice(b * cols, (b + 1) * cols)
            source, start = (out_full, c * sub) if b == 3 else (flat, (3 * c + b) * sub)
            part_a[c, :, lanes] = source[start : start + top, :]
            part_b[c, :, lanes] = source[start + top : start + sub, :]
    split_halves(part_a, kept_a, sent_a, 0, info[3])
    split_halves(part_b, kept_b, sent_b, 1, info[3])


def finish_body(info, kept_a, got_a, kept_b, got_b, qkv, out):
    total = jnp.concatenate(
        [wide(kept_a[...]) + wide(got_a[...]), wide(kept_b[...]) + wide(got_b[...])], axis=0
    )
    cols = out.shape[1]
    turned = [total[:, b * cols : (b + 1) * cols].T for b in range(3)]
    qkv[...] = jnp.concatenate(turned, axis=1)
    out[...] = total[:, 3 * cols :]


def vectors_body(info, one, mid, q_sum, v_sum, cot_a, cot_b, kept, sent, spread):
    me = info[0]
    cols = q_sum.shape[1]
    cot = 0.25 * (cot_a[...] + cot_b[...])
    spread[...] = jnp.zeros_like(spread)
    for d in range(4):
        lanes = slice(d * cols, (d + 1) * cols)
        spread[d, 0:2, :] = one[:, lanes]
        spread[d, 2:5, :] = mid[:, lanes]
        spread[d, 7:8, :] = cot[:, lanes]
    row = lax.broadcasted_iota(jnp.int32, (2, cols), 0)
    spread[me >> 1, 5:7, :] = jnp.where(row == (me & 1), q_sum[...], 0.0)
    spread[2 + (me >> 1), 5:7, :] = jnp.where(row == (me & 1), v_sum[...], 0.0)
    for i in range(2):
        kept[i] = spread[me ^ (2 * i)]
        sent[i] = spread[me ^ (2 * i + 1)]


def norm_two_back_body(info, kept, beside, far, resid, cot, vecs, grad_mid, mid_low, sums):
    block = resid.shape[0]
    grad_second = kept[:block, :] + wide(beside[:block, :]) + wide(far[...])
    normed, inv = norm_stats(resid[...])
    grad = wide(cot[...]) + norm_backward(grad_second, normed, inv, vecs[3:4, :])
    grad_mid[...] = grad
    mid_low[...] = low(grad)
    sums[0:1, :] = jnp.sum(grad, axis=0, keepdims=True)
    sums[1:2, :] = jnp.sum(grad_second * normed, axis=0, keepdims=True)
    sums[2:3, :] = jnp.sum(grad_second, axis=0, keepdims=True)


def value_back_body(
    info, g0, g1, g2, g3, w_out, probs, first, gs, grad_v, v_sum, o0, o1, o2, o3, mid, vacc, flat, pieces
):
    me = info[0]
    block = g0.shape[0]
    heads, rows, dim = gs.shape
    cols = heads * dim
    for r, g in enumerate((g0, g1, g2, g3)):
        mid[r * block : (r + 1) * block, :] = g[...]
    grad_mixed = low(dot(mid[...], w_out[...], NT))
    for h in range(heads):
        gs[h] = grad_mixed[:, h * dim : (h + 1) * dim]

    def one(h, carry):
        vacc[h] = dot(probs[h], gs[h], TN)
        return carry

    lax.fori_loop(0, heads, one, 0)
    grad = jnp.concatenate([vacc[h] for h in range(heads)], axis=1)
    v_sum[...] = jnp.sum(grad, axis=0, keepdims=True)
    grad_v[...] = low(grad)
    flat[...] = low(dot(grad_v[...], first[...], TN))
    for d in range(4):
        pieces[me ^ d] = flat[:, d * cols : (d + 1) * cols]
    for r, out in enumerate((o0, o1, o2, o3)):
        out[...] = pieces[r]


def query_back_body(info, gs, vs, ks, qs, probs, grad_q, grad_k, q_sum, qacc, kacc):
    heads, rows, dim = gs.shape
    scale = 1.0 / math.sqrt(dim)
    step = 256
    kacc[...] = jnp.zeros_like(kacc)

    def one(i, carry):
        h = i // (rows // step)
        start = pl.multiple_of((i % (rows // step)) * step, step)
        here = pl.ds(start, step)
        g = gs[h, here, :]
        share = wide(probs[h, here, :])
        dprob = dot(g, vs[h], NT)
        delta = jnp.sum(share * dprob, axis=-1, keepdims=True)
        dscore = low(share * (dprob - delta) * scale)
        qacc[h, here, :] = dot(dscore, ks[h], NN)
        kacc[h] += dot(dscore, qs[h, here, :], TN)
        return carry

    lax.fori_loop(0, heads * (rows // step), one, 0, unroll=2)
    grad = jnp.concatenate([qacc[h] for h in range(heads)], axis=1)
    q_sum[...] = jnp.sum(grad, axis=0, keepdims=True)
    grad_q[...] = low(grad)
    grad_k[...] = low(jnp.concatenate([kacc[h] for h in range(heads)], axis=1))


def pieces_body(info, grad_a, grad_b, first, o0, o1, o2, o3, flat, pieces):
    me = info[0]
    cols = grad_a.shape[1]
    half = cols // 2
    for j, grad in enumerate((grad_a, grad_b)):
        flat[...] = low(dot(grad[...], first[...], TN))
        for d in range(4):
            for t in range(2):
                pieces[me ^ d, :, (2 * j + t) * cols : (2 * j + t + 1) * cols] = flat[
                    t * half : (t + 1) * half, d * cols : (d + 1) * cols
                ]
    for r, out in enumerate((o0, o1, o2, o3)):
        out[...] = pieces[r]


def first_back_body(info, grad_q, grad_k, grad_v, wq, x0, x1, x2, x3, kept, sent, sums):
    cols = grad_q.shape[1]
    block = x0.shape[0]
    total = None
    for j, grad in enumerate((grad_q, grad_k, grad_v)):
        term = dot(grad[...], wq[:, j * cols : (j + 1) * cols], NT)
        total = term if total is None else total + term
    gain = shift = 0.0
    for r, x in enumerate((x0, x1, x2, x3)):
        part = total[r * block : (r + 1) * block, :]
        normed, _ = norm_stats(wide(x[...]))
        gain = gain + jnp.sum(part * normed, axis=0, keepdims=True)
        shift = shift + jnp.sum(part, axis=0, keepdims=True)
        place = slice((r // 2) * block, (r // 2 + 1) * block)
        if r % 2:
            sent[place, :] = low(part)
        else:
            kept[place, :] = part
    sums[0:1, :] = gain
    sums[1:2, :] = shift


def norm_one_back_body(info, kept, beside, far, x, grad_mid, vecs, out):
    block = x.shape[0]
    normed, inv = norm_stats(wide(x[...]))
    grad_first = kept[:block, :] + wide(beside[:block, :]) + wide(far[...])
    out[...] = low(grad_mid[...] + norm_backward(grad_first, normed, inv, vecs[0:1, :]))


def scatter_near(kept, sent, *others):
    block = kept.shape[0] // 2
    beside = swap(sent, "grp", 1)
    far = low(kept[block:] + wide(beside[block:]))
    return beside, swap(after(far, *others) if others else far, "grp", 2)


def after(values, *others):
    return lax.optimization_barrier((values,) + others)[0]


def rep_bits():
    return lax.axis_size("rep").bit_length() - 1


def rep_label():
    position = lax.axis_index("rep")
    return position ^ ((position >> 1) & (1 << (rep_bits() - 2)))


def rep_swap(values, level):
    top = rep_bits() - 1
    return swap(values, "rep", (3 << (top - 1)) if level == top else (1 << level))


def halve_open(kept, got, order):
    left = sorted(order)
    left.remove(order[0])
    shape = (2,) * len(left) + kept.shape[1:]
    return kept.reshape(shape), got.reshape(shape), left, list(order[1:])


def halve_next(state):
    kept, got, left, order = state
    if not order:
        return state
    level = order[0]
    mine = (rep_label() >> level) & 1
    axis = len(left) - 1 - left.index(level)

    def pick(values, bit):
        return wide(lax.dynamic_index_in_dim(values, bit, axis, keepdims=False))

    got_next = rep_swap(low(pick(kept, 1 - mine) + pick(got, 1 - mine)), level)
    kept = pick(kept, mine) + pick(got, mine)
    return kept, got_next, [x for x in left if x != level], order[1:]


def halve_after(state, *others):
    return (state[0], after(state[1], *others)) + state[2:]


def halve_rest(state):
    while state[3]:
        state = halve_next(state)
    return state[0], state[1]


def on_device(
    block_input,
    lengths,
    ln1_gain,
    ln1_bias,
    w_qkv,
    b_qv,
    w_out,
    b_out,
    ln2_gain,
    ln2_bias,
    w_up,
    b_up,
    w_down,
    b_down,
    cotangent,
):
    images, block, width = block_input.shape
    group = lax.axis_size("grp")
    assert images == 1 and group == 4
    me = lax.axis_index("grp")
    order = me ^ jnp.arange(group)
    cols = width // group
    heads = HEADS // group
    dim = width // HEADS
    rows = group * block
    hidden = w_up.shape[1]
    info = jnp.stack(
        [me.astype(jnp.int32), lengths[0], lax.axis_index("rep").astype(jnp.int32)]
        + [rep_label().astype(jnp.int32)]
    )

    x_near = gather_near(block_input.reshape(block, width))
    half = cols // 2
    w_own, w_beside, w_far = local_call(
        split_w_body,
        [((cols, 3 * cols), BF), ((cols + half, 3 * cols), BF), ((half, 3 * cols), BF)],
        [info, after(w_qkv, x_near[1])],
        [pltpu.VMEM((group, cols, 3 * cols), BF)],
        name="split_w",
        cost=40_000_000,
    )
    small = [after(ln1_gain, w_own), ln1_bias, b_out, ln2_gain, ln2_bias, b_down]
    packed = jnp.concatenate([wide(v) for v in small] + [wide(b_qv)]).reshape(8, cols)
    packed_near = gather_near(packed)
    w_beside = swap(w_beside, "grp", 1)
    w_across = swap(
        after(jnp.concatenate([w_far, w_beside[cols:]]), x_near[2], packed_near[2]), "grp", 2
    )
    vecs, qv_bias = local_call(
        unpack_body,
        [((8, width), F32), ((2, cols), F32)],
        [info] + packed_near,
        [pltpu.VMEM((group, 8, cols), F32)],
        name="unpack",
    )
    cot_near = gather_near(cotangent.reshape(block, width))
    side = lax.axis_index("rep") & 1
    out_half = swap(lax.dynamic_slice_in_dim(w_out, side * half, half, 0), "grp", 2)
    out_other = swap(out_half, "rep", 1)
    out_near = [w_out, swap(w_out, "grp", 1), out_half, out_other]
    out_near += [swap(out_half, "grp", 1), swap(out_other, "grp", 1)]

    (first,) = local_call(
        norm_one_body, [((rows, width), BF)], [info] + x_near + [vecs], name="norm_one"
    )
    w_across, first = lax.optimization_barrier((w_across, first))
    w_near = [w_own, w_beside, w_across, swap(w_across, "rep", 1)]
    head_shape = ((heads, rows, dim), BF)
    wq, qs, ks, vs, probs, mixed = local_call(
        attend_body,
        [((width, 3 * cols), BF), head_shape, head_shape, head_shape]
        + [((heads, rows, rows), BF), ((block, width), BF)],
        [info, first] + w_near + [qv_bias],
        [pltpu.VMEM((heads, rows, dim), BF)],
        name="attend",
    )

    mixed_near = gather_near(mixed)

    def mlp(blocks, keep):
        kind = F32 if keep else BF
        outs = [((2 * block, width), BF), ((2 * block, hidden), BF), ((2 * block, hidden), BF)]
        outs += [((2 * block, width), kind)]
        outs += [((1, hidden), F32), ((1, width), F32)]
        if keep:
            outs += [((block, width), F32)]
        args = [info] + mixed_near + out_near + [x_near[b] for b in blocks]
        args += [cot_near[b] for b in blocks] + [vecs, w_up.T, b_up.reshape(1, -1), w_down]
        return local_call(
            functools.partial(mlp_body, blocks, keep),
            outs,
            args,
            [pltpu.VMEM((2 * cols, width), BF)],
            name="mlp",
        )

    size = lax.axis_size("rep")
    forth = list(range(rep_bits()))
    turned = [1, 0] + forth[2:]
    inner = [1, forth[-1], 0] + forth[2:-1]

    def weight_grad(a, b, level, name):
        wide_rows, n = a[0].shape[1], b[0].shape[1]
        chunk = wide_rows // size
        half = ((size // 2, chunk, n), BF)
        return local_call(
            functools.partial(weight_body, level),
            [half, half],
            [info] + a + b,
            [pltpu.VMEM((size, chunk, n), BF)],
            name=name,
        )

    second_s, act_s, gate_s, back_s, gsum_s, csum_s = mlp((1, 3), False)
    second_k, act_k, gate_k, back_k, gsum_k, csum_k, resid_own = mlp((0, 2), True)
    beside, far = scatter_near(back_k, back_s)
    cots = [cot_near[b] for b in (1, 3, 0, 2)]
    down_kept, down_sent = weight_grad(cots, [act_s, act_k], 0, "down_grad")
    down_got = swap(down_sent, "rep", 1)
    up_kept, up_sent = weight_grad([second_s, second_k], [gate_s, gate_k], 1, "up_grad")
    up_got = swap(up_sent, "rep", 2)
    grad_mid, mid_low, mid_sums = local_call(
        norm_two_back_body,
        [((block, width), F32), ((block, width), BF), ((3, width), F32)],
        [info, back_k, beside, after(far, down_kept, up_kept), resid_own, cot_near[0], vecs],
        name="norm_two_back",
    )
    mid_across = swap(mid_low, "grp", 2)
    fwd_s, fwd_k = local_call(
        forward_body,
        [((2 * block, width), BF), ((2 * block, width), F32)],
        [info, after(act_s, mid_low), act_k, w_down],
        name="forward",
    )
    mid_across, fwd_s = lax.optimization_barrier((mid_across, fwd_s))
    mid_near = [mid_low, swap(mid_low, "grp", 1), mid_across, swap(mid_across, "grp", 1)]

    gs, grad_v, v_sum, *v_pieces = local_call(
        value_back_body,
        [head_shape, ((rows, cols), BF), ((1, cols), F32)] + [((cols, cols), BF)] * group,
        [info] + mid_near + [w_out, probs, first],
        [
            pltpu.VMEM((rows, width), BF),
            pltpu.VMEM((heads, rows, dim), F32),
            pltpu.VMEM((cols, width), BF),
            pltpu.VMEM((group, cols, cols), BF),
        ],
        name="value_back",
    )

    down_state = halve_open(down_kept, down_got, forth)
    up_state = halve_open(up_kept, up_got, inner)
    gs, down_now, up_now = lax.optimization_barrier((gs, down_state[1], up_state[1]))
    down_state = halve_next((down_state[0], down_now) + down_state[2:])
    up_state = halve_next((up_state[0], up_now) + up_state[2:])

    def exchange(pieces):
        return [pieces[0]] + [swap(pieces[r], "grp", r) for r in range(1, group)]

    v_got = exchange(v_pieces)
    grad_q, grad_k, q_sum = local_call(
        query_back_body,
        [((rows, cols), BF), ((rows, cols), BF), ((1, cols), F32)],
        [info, gs, vs, ks, qs, probs],
        [pltpu.VMEM((heads, rows, dim), F32)] * 2,
        name="query_back",
    )
    up_now = up_state[1]
    grad_k, down_now, *v_got = lax.optimization_barrier((grad_k, down_state[1], *v_got))
    qk_pieces = local_call(
        pieces_body,
        [((half, width), BF)] * group,
        [info, grad_q, grad_k, first],
        [pltpu.VMEM((cols, width), BF), pltpu.VMEM((group, half, width), BF)],
        name="qk_pieces",
    )
    qk_got = exchange(qk_pieces)
    down_now = after(down_now, qk_pieces[0])
    down_state = halve_next((down_state[0], down_now) + down_state[2:])
    first_k, first_s, one_sums = local_call(
        first_back_body,
        [((2 * block, width), F32), ((2 * block, width), BF), ((2, width), F32)],
        [info, after(grad_q, qk_pieces[0], down_state[0]), grad_k, grad_v, wq] + x_near,
        name="first_back",
    )
    vec_kept, vec_sent = local_call(
        vectors_body,
        [((2, 8, cols), F32)] * 2,
        [info, one_sums, mid_sums, q_sum, v_sum, csum_s, csum_k],
        [pltpu.VMEM((group, 8, cols), F32)],
        name="vectors",
    )
    (out_full,) = local_call(
        out_grad_body,
        [((width, cols), BF)],
        [info] + mid_near + [after(mixed, first_s, vec_sent)],
        name="out_grad",
    )
    down_now, up_now, out_full = lax.optimization_barrier((down_state[1], up_state[1], out_full))
    down_state = (down_state[0], down_now) + down_state[2:]
    up_state = (up_state[0], up_now) + up_state[2:]
    sub = width // size
    top = sub // 32 * 16
    halves = [((size // 2, top, width), BF)] * 2 + [((size // 2, sub - top, width), BF)] * 2
    a_kept, a_sent, b_kept, b_sent = local_call(
        assemble_body,
        halves,
        [info] + v_got + qk_got + [out_full],
        [pltpu.VMEM((3 * width, cols), BF), pltpu.VMEM((size, top, width), BF)]
        + [pltpu.VMEM((size, sub - top, width), BF)],
        name="assemble",
    )
    a_state = halve_open(a_kept, swap(a_sent, "rep", 1), forth)
    b_state = halve_open(b_kept, swap(b_sent, "rep", 2), turned)
    up_state = halve_next(halve_after(up_state, a_sent, b_sent))
    first_beside, first_far = scatter_near(first_k, after(first_s, a_sent, b_sent))
    pair = vec_kept + swap(after(vec_sent, a_sent, b_sent), "grp", 1)
    fwd_beside, fwd_far = scatter_near(fwd_k, after(fwd_s, a_sent, b_sent))
    mine = pair[0] + swap(pair[1], "grp", 2)
    up_bias = jnp.pad(gsum_s + gsum_k, ((0, 0), (0, -hidden % cols))).reshape(-1, cols)
    mine = jnp.concatenate([mine, up_bias])
    for level in range(rep_bits()):
        mine_got, a_now, b_now, first_far = lax.optimization_barrier(
            (rep_swap(mine, level), a_state[1], b_state[1], first_far)
        )
        a_state = halve_next((a_state[0], a_now) + a_state[2:])
        b_state = halve_next((b_state[0], b_now) + b_state[2:])
        mine = mine + mine_got
        if level == 0:
            down_state = halve_after(down_state, a_now)
            up_state = halve_after(up_state, a_now)
            (grad_rows,) = local_call(
                norm_one_back_body,
                [((block, width), BF)],
                [info, first_k, first_beside, first_far, x_near[0], grad_mid, vecs],
                name="norm_one_back",
            )
    block_rows = resid_own + (fwd_k[:block] + wide(fwd_beside[:block]) + wide(fwd_far) + vecs[5])
    down_kept, down_got = halve_rest(down_state)
    down_grad = wide(down_kept) + wide(down_got)
    up_kept, up_got = halve_rest(up_state)
    up_grad = wide(up_kept) + wide(up_got)
    qkv_grad, out_grad = local_call(
        finish_body,
        [((cols, 3 * sub), F32), ((sub, cols), F32)],
        [info, *halve_rest(a_state), *halve_rest(b_state)],
        name="finish",
    )

    return (
        low(block_rows).reshape(block_input.shape),
        grad_rows.reshape(block_input.shape),
        mine[0],
        mine[1],
        qkv_grad,
        mine[5:7].reshape(-1),
        out_grad.T,
        mine[2],
        mine[3],
        mine[4],
        up_grad,
        mine[8:].reshape(-1)[:hidden],
        down_grad.T,
        mine[7],
    )


def solution(mesh):
    in_specs = (
        P("rep", "grp", None),
        P("rep"),
        P("grp"),
        P("grp"),
        P("grp", None),
        P("grp"),
        P("grp", None),
        P("grp"),
        P("grp"),
        P("grp"),
        P(None, "grp"),
        P("grp"),
        P("grp", None),
        P("grp"),
        P("rep", "grp", None),
    )
    out_specs = (
        P("rep", "grp", None),
        P("rep", "grp", None),
        P("grp"),
        P("grp"),
        P("grp", "rep"),
        P("grp"),
        P("grp", "rep"),
        P("grp"),
        P("grp"),
        P("grp"),
        P("rep", "grp"),
        P("grp"),
        P("grp", "rep"),
        P("grp"),
    )
    return jax.shard_map(
        on_device, mesh=mesh, in_specs=in_specs, out_specs=out_specs, check_vma=False
    )
```
